256 devices in a mesh: dap: 128 (over y, x, z_hi, core), dp: 2 (over z_lo).
Axes of the slice: x: 4, y: 4, z: 8 (z_hi: 4, z_lo: 2; z = z_hi * 2 + z_lo), core: 2. Of those that a mesh axis runs over, the one named last changes fastest.
Arguments:
- pair: bfloat16 [512, 256, 128], P(('dp', 'dap')), parts along dimension 0
- token_mask: int32 [512], P('dp'), parts along dimension 0, may hold values from 0 to 1, as said below
- chain_ids: int32 [512], P('dp'), parts along dimension 0, may hold values from 0 to 3, never falling along the last dimension, each value on 1 to 128 neighbouring positions
- proj_weight: bfloat16 [128, 512], replicated
- bias_weight: bfloat16 [128, 4], replicated, may hold values from -0.5 to 0.5
- chain_weight: float32 [4], replicated, may hold values from -1.5 to 1.5
- out_weight: bfloat16 [128, 128], replicated, may hold values from -0.5 to 0.5
- cotangent: bfloat16 [512, 256, 128], P(('dp', 'dap')), parts along dimension 0, may hold values from -24 to 24
Outputs:
- next_pair_t: float32 [512, 256, 128], P(('dp', 'dap')), parts along dimension 0
- pair_grad: bfloat16 [512, 256, 128], P(('dp', 'dap')), parts along dimension 0
- proj_grad: float32 [256, 512], P('dp'), parts along dimension 0
- bias_weight_grad: float32 [256, 4], P('dp'), parts along dimension 0
- chain_grad: float32 [8], P('dp'), parts along dimension 0
- out_grad: float32 [256, 128], P('dp'), parts along dimension 0
The draws below stay inside these ranges and needn't reach their ends.
There are 2 independent parts, one for each index of `dp`. The reference program is written for one: setup_inputs(seed, part) draws one part's arguments, and reference() takes and returns one part's arrays. A program takes and returns all parts, laid end to end along the dimension named above; an argument that names none is the same for every part. Nothing has to cross between parts.
Inputs may be any that keep to these rules, and one draw needn't show every extreme that they name: `token_mask`: tokens are real up to some point and padding after it; the first 128 tokens are real and the last token is padding. `chain_ids`: chain numbers never fall along the tokens; every chain has 1 to 128 tokens, one chain exactly 128.
All inputs are finite; a program needn't handle non-finite values.
Results may differ from the reference program's by a relative error of at most 0.011.
Values may be sent and summed in bfloat16 or wider, within the bound.
A program may use at most 64 MiB of HBM per device.

```python
import math
import jax
import jax.numpy as jnp
import numpy as np
from jax import lax

C = 128
H = 4
DH = 32
HD = 128
N = 256


def draw_pair(key, part):
    first_key = jax.random.fold_in(jax.random.fold_in(key, 11), 0)
    values_f = jax.random.normal(first_key, (N, N, C), jnp.float32)
    return values_f.astype(jnp.bfloat16)


def draw_proj_weight(key, part):
    keys_list = jax.random.split(jax.random.fold_in(key, 23), 1)
    drawn_part = jax.random.normal(keys_list[0], (C, 4 * HD), jnp.float32) * C ** (-0.5)
    values_f = drawn_part
    return values_f.astype(jnp.bfloat16)


def draw_token_mask(key, part):
    real_count = jax.random.randint(jax.random.fold_in(key, 5), (), N // 2, N)
    return (jnp.arange(N) < real_count).astype(jnp.int32)


def strengthened(array, key, source, target, blocks, factor):
    def block_of(axis_at):
        return (jnp.arange(array.shape[axis_at]) // (array.shape[axis_at] // blocks)).reshape((-1,) + (1,) * (array.ndim - 1 - axis_at))

    near = jax.random.permutation(key, blocks)[block_of(target)]
    other_side = (block_of(target) + blocks // 2) % blocks
    return jnp.where((block_of(source) == near) | (block_of(source) == other_side), factor * array, array)


def shard_levels(own_key, extent, cuts, low, top_value):
    level = 1.0
    for axis_at, blocks in cuts:
        heights = jax.random.uniform(jax.random.fold_in(jax.random.fold_in(own_key, 6), axis_at), (blocks,), jnp.float32, low / len(cuts), top_value / len(cuts))
        level = level * jnp.repeat(jnp.exp(heights), extent[axis_at] // blocks).reshape((-1,) + (1,) * (len(extent) - 1 - axis_at))
    return level


def split_up(number_of, total, reach, lean):
    weights = [(1 << 20) // math.isqrt(standing ** lean) + 1 for standing in range(2, number_of + 1)]
    spare, given = total - reach - (number_of - 1), [1] * (number_of - 1)
    while spare > 0:
        candidates = [i for i in range(number_of - 1) if given[i] < reach]
        whole, remaining = sum([weights[i] for i in candidates]), spare
        for i in candidates:
            more = min(reach - given[i], max(1, remaining * weights[i] // whole), spare)
            given[i] = given[i] + more
            spare = spare - more
    return np.array([reach] + given)


def uneven(key, amount, total, reach, skew):
    if amount == 2:
        one = jax.random.randint(key, (), max(1, total - reach), min(reach, total - 1) + 1)
        return jnp.stack([one, total - one])
    lengths = jnp.asarray(split_up(amount, total, reach, skew), jnp.int32)
    couples = (amount - 1) // 2
    source_of, taker = lengths[1:1 + 2 * couples:2], lengths[2:2 + 2 * couples:2]
    margin = jnp.minimum(source_of - 1, reach - taker)
    moved = jax.random.randint(jax.random.fold_in(key, 1), (couples,), 0, 1 << 20) % (margin + 1)
    lengths = lengths.at[1:1 + 2 * couples:2].set(source_of - moved).at[2:2 + 2 * couples:2].set(taker + moved)
    return lengths[jax.random.permutation(jax.random.fold_in(key, 2), amount)]


def noise(rng, extent, scale, bound, cuts=(), held_as=jnp.bfloat16):
    array = scale * jax.random.normal(rng, extent, jnp.float32)
    if cuts:
        array = array * shard_levels(rng, extent, cuts, -0.22, 0.18)
    return jnp.clip(array, -bound, bound).astype(held_as)


def gaussian_with(key, extent, width, reach, cuts, heavy, dtype=jnp.bfloat16):
    result = width * jax.random.normal(key, extent, jnp.float32)
    if cuts:
        result = result * shard_levels(key, extent, cuts, -0.22, 0.18)
    return jnp.clip(strengthened(result, jax.random.fold_in(key, 3), *heavy), -reach, reach).astype(dtype)


def setup_inputs(seed: int = 0, part: int = 0) -> dict:
    key_list = jax.random.split(jax.random.key(seed), 9)
    part_splits = jax.random.split(jax.random.fold_in(key_list[8], part), 9)
    return {
        "pair": draw_pair(jax.random.fold_in(jax.random.fold_in(key_list[8], part), 71), part),
        "token_mask": draw_token_mask(jax.random.fold_in(jax.random.fold_in(key_list[8], part), 71), part),
        "chain_ids": jnp.searchsorted(jnp.cumsum(uneven(part_splits[2], 4, N, N // 2, 1)), jnp.arange(N), side="right").astype(jnp.int32),
        "proj_weight": draw_proj_weight(jax.random.fold_in(key_list[8], 71), part),
        "bias_weight": noise(key_list[4], (C, H), C ** -0.5, 0.5),
        "chain_weight": jnp.clip(jax.random.uniform(key_list[5], (H,), jnp.float32, -1.5, 1.5), -1.5, 1.5),
        "out_weight": noise(key_list[6], (HD, C), HD ** -0.5, 0.5),
        "cotangent": gaussian_with(part_splits[7], (N, N, C), 1.0, 24.0, ((0, 128),), (0, 1, 128, 5.5)),
    }


epsilon = 1e-05
contract_rows = (((0,), (0,)), ((), ()))
contract_cols = (((1,), (1,)), ((), ()))

def normalize(pair):
    values_f = pair.astype(jnp.float32)
    centered = values_f - lax.optimization_barrier(jnp.mean(values_f, axis=-1, keepdims=True))
    inverse = lax.rsqrt(lax.optimization_barrier(jnp.mean(centered * centered, axis=-1, keepdims=True)) + epsilon)
    return (centered * inverse, inverse)

def row_softmax(query_row, key_row, bias_head, extra_head):
    scores = lax.dot_general(query_row, key_row, contract_cols, preferred_element_type=jnp.float32)
    scores = scores + bias_head.astype(jnp.float32) + extra_head
    highest = lax.optimization_barrier(jnp.max(scores, axis=1, keepdims=True))
    expo_s = jnp.exp(scores - highest)
    return expo_s / lax.optimization_barrier(jnp.sum(expo_s, axis=1, keepdims=True))

def forward_rows(query_h, key_h, value_h, bias_head, extra_head):

    def one_row(items):
        query_row, key_row, value_row = items
        attention = row_softmax(query_row, key_row, bias_head, extra_head)
        return jnp.dot(attention.astype(jnp.bfloat16), value_row, preferred_element_type=jnp.float32)
    return lax.map(one_row, (query_h, key_h, value_h))

def backward_rows(query_h, key_h, value_h, grad_h, bias_head, extra_head):

    def one_row(summed, items):
        query_row, key_row, value_row, grad_row = items
        attention = row_softmax(query_row, key_row, bias_head, extra_head)
        d_probs = lax.dot_general(grad_row, value_row, contract_cols, preferred_element_type=jnp.float32)
        inner_sum = lax.optimization_barrier(jnp.sum(attention * d_probs, axis=1, keepdims=True))
        d_scores = attention * (d_probs - inner_sum)
        scores_low = d_scores.astype(jnp.bfloat16)
        d_query = jnp.dot(scores_low, key_row, preferred_element_type=jnp.float32)
        d_key = lax.dot_general(scores_low, query_row, contract_rows, preferred_element_type=jnp.float32)
        d_value = lax.dot_general(attention.astype(jnp.bfloat16), grad_row, contract_rows, preferred_element_type=jnp.float32)
        return (summed + d_scores, (d_query, d_key, d_value))
    tokens = bias_head.shape[1]
    return lax.scan(one_row, jnp.zeros((tokens, tokens), jnp.float32), (query_h, key_h, value_h, grad_h))

def reference(pair, token_mask, chain_ids, proj_weight, bias_weight, chain_weight, out_weight, cotangent):
    standard, inverse = normalize(pair)
    normed = standard.astype(jnp.bfloat16)
    flat_x = normed.reshape(N * N, C)
    projected = jnp.dot(flat_x, proj_weight, preferred_element_type=jnp.float32).reshape(N, N, 4 * HD)
    scaling = DH ** (-0.5)
    query = (projected[..., :HD] * scaling).astype(jnp.bfloat16)
    key_rows = projected[..., HD:2 * HD].astype(jnp.bfloat16)
    value_rows = projected[..., 2 * HD:3 * HD].astype(jnp.bfloat16)
    gating = jax.nn.sigmoid(projected[..., 3 * HD:])
    pair_bias = jnp.dot(flat_x, bias_weight, preferred_element_type=jnp.float32).reshape(N, N, H)
    pair_bias = jnp.transpose(pair_bias, (2, 0, 1)).astype(jnp.bfloat16)
    same_chain = (chain_ids[:, None] == chain_ids[None, :]).astype(jnp.float32)
    masked = (token_mask.astype(jnp.float32) - 1.0) * 1000000000.0
    outputs = []
    for number in range(H):
        columns = slice(number * DH, (number + 1) * DH)
        extra_head = chain_weight[number] * same_chain + masked[None, :]
        outputs.append(forward_rows(query[:, :, columns], key_rows[:, :, columns], value_rows[:, :, columns], pair_bias[number], extra_head))
    attended = jnp.concatenate(outputs, axis=-1)
    gated = (gating * attended).astype(jnp.bfloat16)
    gated_flat = gated.reshape(N * N, HD)
    update = jnp.dot(gated_flat, out_weight, preferred_element_type=jnp.float32).reshape(N, N, C)
    next_pair_t = jnp.transpose(pair.astype(jnp.float32) + update, (1, 0, 2))
    grad_flat = cotangent.reshape(N * N, C)
    out_grad = lax.dot_general(gated_flat, grad_flat, contract_rows, preferred_element_type=jnp.float32) / N
    d_gated = lax.dot_general(grad_flat, out_weight, contract_cols, preferred_element_type=jnp.float32).reshape(N, N, HD)
    d_attended = (d_gated * gating).astype(jnp.bfloat16)
    d_gate = d_gated * attended * gating * (1.0 - gating)
    query_parts, key_parts, value_parts, sums_list = ([], [], [], [])
    for number in range(H):
        columns = slice(number * DH, (number + 1) * DH)
        extra_head = chain_weight[number] * same_chain + masked[None, :]
        summed, (d_query, d_key, d_value) = backward_rows(query[:, :, columns], key_rows[:, :, columns], value_rows[:, :, columns], d_attended[:, :, columns], pair_bias[number], extra_head)
        query_parts.append(d_query)
        key_parts.append(d_key)
        value_parts.append(d_value)
        sums_list.append(summed)
    bias_total = jnp.stack(sums_list, axis=-1)
    d_proj = jnp.concatenate([jnp.concatenate(query_parts, axis=-1) * scaling, jnp.concatenate(key_parts, axis=-1), jnp.concatenate(value_parts, axis=-1), d_gate], axis=-1).astype(jnp.bfloat16)
    d_bias = bias_total.astype(jnp.bfloat16)
    d_proj_flat = d_proj.reshape(N * N, 4 * HD)
    d_bias_flat = d_bias.reshape(N * N, H)
    d_normed = lax.dot_general(d_proj_flat, proj_weight, contract_cols, preferred_element_type=jnp.float32)
    d_normed = d_normed + lax.dot_general(d_bias_flat, bias_weight, contract_cols, preferred_element_type=jnp.float32)
    d_normed = d_normed.reshape(N, N, C)
    mean_grad = lax.optimization_barrier(jnp.mean(d_normed, axis=-1, keepdims=True))
    mean_cross = lax.optimization_barrier(jnp.mean(d_normed * standard, axis=-1, keepdims=True))
    pair_grad = ((d_normed - mean_grad - standard * mean_cross) * inverse).astype(jnp.bfloat16)
    proj_grad = lax.dot_general(flat_x, d_proj_flat, contract_rows, preferred_element_type=jnp.float32) / N
    bias_weight_grad = lax.dot_general(flat_x, d_bias_flat, contract_rows, preferred_element_type=jnp.float32) / N
    chain_grad = lax.optimization_barrier(jnp.sum(bias_total * same_chain[:, :, None], axis=(0, 1))) / N
    return (next_pair_t, pair_grad, proj_grad, bias_weight_grad, chain_grad, out_grad)
```

```python
import functools

import jax
import jax.numpy as jnp
from jax import lax
from jax.experimental import pallas as pl
from jax.experimental.pallas import tpu as pltpu
from jax.sharding import PartitionSpec as P

H = 4
DH = 32
HD = 128
C = 128
GRID = (4, 4, 4, 2)
EPSILON = 1e-05

F32 = jnp.float32
BF16 = jnp.bfloat16
NN = (((1,), (0,)), ((), ()))
NT = (((1,), (1,)), ((), ()))
TN = (((0,), (0,)), ((), ()))


def dot(a, b, dims=NN):
    return lax.dot_general(a, b, dims, preferred_element_type=F32)


def kernel(
    grid,
    tokens,
    cw_ref,
    pair_ref,
    mask_ref,
    chain_ref,
    w_ref,
    bw_ref,
    ow_ref,
    cot_ref,
    npt_ref,
    pg_ref,
    wg_ref,
    small_ref,
    std_ref,
    inv_ref,
    normed_ref,
    q_ref,
    k_ref,
    v_ref,
    da_ref,
    qt_ref,
    dat_ref,
    gate_ref,
    dgated_ref,
    att_ref,
    dq_ref,
    dkt_ref,
    dvt_ref,
    same_ref,
    dbias_ref,
    dproj_ref,
    slot_ref,
    bias_ref,
    sc_ref,
    rc_ref,
    sa_ref,
    ra_ref,
    sb_ref,
    rb_ref,
    sz_ref,
    rz_ref,
    wsc_ref,
    wrc_ref,
    wsa_ref,
    wra_ref,
    wrb_ref,
    wrz_ref,
    wag_ref,
    us_ref,
    ua_ref,
    ub_ref,
    ux_ref,
    uz_ref,
    ur_ref,
    t0_ref,
    t1_ref,
    t2_ref,
    slot_s,
    slot_r,
    ag_s,
    ag_r,
    agc_s,
    agc_r,
    rsc_s,
    rsc_r,
    rsa_s,
    rsa_r,
    rsb_s,
    rsb_r,
    rsz_s,
    rsz_r,
    wc_s,
    wc_r,
    wa_s,
    wa_r,
    wb_s,
    wb_r,
    wz_s,
    wz_r,
    wga_s,
    wga_r,
    wgc_s,
    wgc_r,
    ua_s,
    ua_r,
    ub_s,
    ub_r,
    uz_s,
    uz_r,
    t0_s,
    t0_r,
    t1_s,
    t1_r,
    t2_s,
    t2_r,
):
    NY, NX, NZ, NC = grid
    G = NZ * NC
    NB = NX * NY
    NA = NX
    BR = 2 * G
    N = tokens
    T = 2 * N
    HC = H // NC
    WR = C // NC // NA

    idx = lax.axis_index("dap")
    zc = lax.rem(idx, G)
    c = lax.rem(idx, NC)
    z = lax.div(zc, NC)
    yx = lax.div(idx, G)
    x = lax.rem(yx, NX)
    y = lax.div(yx, NX)
    a_me = x + (y - x) * c
    b_me = y + (x - y) * c
    a_stride = G + (G * NX - G) * c
    b_stride = G * NX - (G * NX - G) * c
    partner = idx + 1 - 2 * c
    far = HC * (1 - c)
    near = HC * c

    def blk(a, b):
        return a * (1 + (NX - 1) * c) + b * (NX - (NX - 1) * c)

    def zc_peer(g):
        return idx + g - zc

    def a_peer(a):
        return idx + (a - a_me) * a_stride

    def b_peer(b):
        return idx + (b - b_me) * b_stride

    def z_peer(zz):
        return idx + (zz - z) * NC

    def x_peer(xx):
        return idx + (xx - x) * G

    def y_peer(yy):
        return idx + (yy - y) * G * NX

    def others(me, n):
        return [lax.rem(me + d, n) for d in range(1, n)]

    def copy(src, dst, ssem, rsem, dev):
        return pltpu.make_async_remote_copy(
            src_ref=src,
            dst_ref=dst,
            send_sem=ssem,
            recv_sem=rsem,
            device_id={"dap": dev},
            device_id_type=pl.DeviceIdType.MESH,
        )

    barrier = pltpu.get_barrier_semaphore()
    peers = [zc_peer(g) for g in others(zc, G)]
    peers += [x_peer(v) for v in others(x, NX)]
    peers += [y_peer(v) for v in others(y, NY)]
    for p in peers:
        pl.semaphore_signal(
            barrier, inc=1, device_id={"dap": p}, device_id_type=pl.DeviceIdType.MESH
        )

    values = pair_ref[...].reshape(T, C).astype(F32)
    centered = values - jnp.mean(values, axis=-1, keepdims=True)
    inverse = lax.rsqrt(jnp.mean(centered * centered, axis=-1, keepdims=True) + EPSILON)
    standard = centered * inverse
    std_ref[...] = standard
    inv_ref[...] = jnp.broadcast_to(inverse, (T, C))
    normed = standard.astype(BF16)
    normed_ref[...] = normed
    bwt = jnp.transpose(bw_ref[...].astype(F32)).astype(BF16)
    local_bias = dot(bwt, normed, NT)
    slot_ref[zc] = jnp.concatenate(
        [local_bias[0:H, 0:N], local_bias[0:H, N:T]], axis=0
    ).astype(BF16)

    pl.semaphore_wait(barrier, len(peers))
    slot_out = []
    for g in others(zc, G):
        d = copy(slot_ref.at[zc], slot_ref.at[zc], slot_s.at[g], slot_r.at[zc], zc_peer(g))
        d.start()
        slot_out.append(d)

    def arrived(ref, sem):
        copy(ref, ref, sem, sem, partner).wait_recv()

    projected = dot(normed, w_ref[...])
    scaling = DH ** (-0.5)
    q = (projected[:, 0:HD] * scaling).astype(BF16)
    q_ref[...] = q
    k_ref[...] = projected[:, HD : 2 * HD].astype(BF16)
    v_ref[...] = projected[:, 2 * HD : 3 * HD].astype(BF16)
    gating = jax.nn.sigmoid(projected[:, 3 * HD :])
    gate_ref[...] = gating

    for g in others(zc, G):
        arrived(slot_ref.at[g], slot_r.at[g])
    gathered = slot_ref[...].reshape(G * 2 * H, N)
    for t in range(HC):
        at = lax.broadcasted_iota(jnp.int32, (BR, G * 2 * H), 0) * H + (far + t)
        pick = (at == lax.broadcasted_iota(jnp.int32, (BR, G * 2 * H), 1)).astype(BF16)
        bias_ref[far + t, yx] = dot(pick, gathered).astype(BF16)

    ag_out = []

    def ag_send(number, block, dev, ssem, rsem):
        part = bias_ref.at[pl.ds(far, HC), block]
        d = copy(part, part, ssem.at[number], rsem.at[block], dev)
        d.start()
        ag_out.append(d)

    number = 0
    for b in others(b_me, NA):
        ag_send(number, yx, b_peer(b), ag_s, ag_r)
        number += 1
    for a in others(a_me, NA):
        ag_send(number, yx, a_peer(a), ag_s, ag_r)
        number += 1
    ag_send(yx, yx, partner, agc_s, agc_r)

    grad = cot_ref[...].reshape(T, C)
    d_gated = dot(grad, ow_ref[...], NT)
    dgated_ref[...] = d_gated
    da32 = d_gated * gating
    da_ref[...] = da32.astype(BF16)
    for r in range(2):
        rows = slice(r * N, (r + 1) * N)
        qt_ref[r] = jnp.transpose(projected[rows, 0:HD] * scaling).astype(BF16)
        dat_ref[r] = jnp.transpose(da32[rows]).astype(BF16)
    chain = chain_ref[...].astype(F32)
    chain_cols = jnp.transpose(jnp.broadcast_to(chain, (HD, N)))
    chain_cols = jnp.concatenate([chain_cols] * (-(-N // HD)), axis=1)[:, 0:N]
    same_ref[...] = (chain_cols == jnp.broadcast_to(chain, (N, N))).astype(F32)

    def landed(block, sem):
        part = bias_ref.at[pl.ds(far, HC), block]
        copy(part, part, sem.at[block], sem.at[block], partner).wait_recv()

    for b in others(b_me, NA):
        block = blk(a_me, b)
        landed(block, ag_r)
        for a in others(a_me, NA):
            ag_send(number, block, a_peer(a), ag_s, ag_r)
            number += 1
        ag_send(block, block, partner, agc_s, agc_r)
    for a in others(a_me, NA):
        for b in range(NA):
            block = blk(a, b)
            landed(block, ag_r)
            ag_send(block, block, partner, agc_s, agc_r)

    masked = (mask_ref[...].astype(F32) - 1.0) * 1000000000.0
    head_of = lax.broadcasted_iota(jnp.int32, (N, HD), 1) // DH
    att_ref[...] = jnp.zeros((2, N, HD), F32)
    dq_ref[...] = jnp.zeros((2, N, HD), F32)

    def one_head(h):
        own = head_of == h
        none = jnp.zeros((N, HD), BF16)
        extra = cw_ref[h] * same_ref[...] + masked
        bias = bias_ref[h].reshape(N, N).astype(F32)
        head_rows = pl.ds(pl.multiple_of(h * DH, DH), DH)
        for r in range(2):
            rows = slice(r * N, (r + 1) * N)
            k_row, v_row = k_ref[rows, :], v_ref[rows, :]
            scores = dot(jnp.where(own, q_ref[rows, :], none), k_row, NT)
            scores = scores + bias + extra
            expo = jnp.exp(scores - jnp.max(scores, axis=1, keepdims=True))
            probs = expo * (1.0 / jnp.sum(expo, axis=1, keepdims=True))
            probs_low = probs.astype(BF16)
            att_ref[r] += dot(probs_low, jnp.where(own, v_row, none))
            d_probs = dot(jnp.where(own, da_ref[rows, :], none), v_row, NT)
            inner = jnp.sum(probs * d_probs, axis=1, keepdims=True)
            d_scores = probs * (d_probs - inner)
            low = d_scores.astype(BF16)
            dq_ref[r] += dot(low, jnp.where(own, k_row, none))
            dkt_ref[r, head_rows, :] = dot(qt_ref[r, head_rows, :], low)
            dvt_ref[r, head_rows, :] = dot(dat_ref[r, head_rows, :], probs_low)
            if r == 0:
                dbias_ref[h] = d_scores
            else:
                dbias_ref[h] += d_scores


    def far_landed():
        for a in range(NA):
            for b in range(NA):
                block = blk(a, b)
                part = bias_ref.at[pl.ds(near, HC), block]
                sem = agc_r.at[block]
                copy(part, part, sem, sem, partner).wait_recv()

    def rsc(t):
        return copy(sc_ref.at[t], rc_ref.at[t], rsc_s.at[t], rsc_r.at[t], partner)

    @pl.loop(0, HC)
    def _(t):
        one_head(far + t)
        sc_ref[t] = dbias_ref[far + t].reshape(NB, BR, N).astype(BF16)
        rsc(t).start()

    far_landed()

    @pl.loop(0, HC)
    def _(t):
        one_head(near + t)

    for t in range(HC):
        rsc(t).wait_recv()
        total = dbias_ref[near + t] + rc_ref[t].reshape(N, N).astype(F32)
        sa_ref[t] = total.reshape(NB, BR, N).astype(BF16)
    rsa_out = []
    number = 0
    for a in others(a_me, NA):
        for b in range(NA):
            d = copy(
                sa_ref.at[:, blk(a, b)],
                ra_ref.at[a_me, b],
                rsa_s.at[number],
                rsa_r.at[a_me * NA + b],
                a_peer(a),
            )
            d.start()
            rsa_out.append(d)
            number += 1

    attended = att_ref[...].reshape(T, HD)
    gating = gate_ref[...]
    gated = (gating * attended).astype(BF16)
    grad = cot_ref[...].reshape(T, C)
    update = dot(gated, ow_ref[...])
    next_pair = pair_ref[...].reshape(T, C).astype(F32) + update
    us_ref[...] = next_pair.astype(BF16).reshape(2, NB, BR, C)
    ua_out = []
    number = 0
    for a in others(a_me, NA):
        for b in range(NA):
            d = copy(
                us_ref.at[:, blk(a, b)],
                ua_ref.at[a_me, b],
                ua_s.at[number],
                ua_r.at[a_me * NA + b],
                a_peer(a),
            )
            d.start()
            ua_out.append(d)
            number += 1

    d_gate = dgated_ref[...] * attended * gating * (1.0 - gating)
    dproj_ref[:, 0:HD] = (dq_ref[...].reshape(T, HD) * scaling).astype(BF16)
    for r in range(2):
        rows = slice(r * N, (r + 1) * N)
        dproj_ref[rows, HD : 2 * HD] = jnp.transpose(dkt_ref[r]).astype(BF16)
        dproj_ref[rows, 2 * HD : 3 * HD] = jnp.transpose(dvt_ref[r]).astype(BF16)
    dproj_ref[:, 3 * HD :] = d_gate.astype(BF16)
    normed = normed_ref[...]
    proj_part = dot(normed, dproj_ref[...], TN)
    out_part = dot(gated, grad, TN)
    half = C // NC
    wfull_ref = wag_ref
    wsum = jnp.concatenate([proj_part, out_part], axis=1).reshape(NC, half, 5 * HD)
    wfull_ref[...] = wsum.astype(BF16).reshape(NC, NA, WR, 5 * HD)
    wsc_ref[...] = wfull_ref[1 - c]
    wc = copy(wsc_ref, wrc_ref, wc_s, wc_r, partner)
    wc.start()

    for b in range(NA):
        arrived_rows = sa_ref[:, blk(a_me, b)].astype(F32)
        for a in others(a_me, NA):
            arrived(ra_ref.at[a, b], rsa_r.at[a * NA + b])
            arrived_rows = arrived_rows + ra_ref[a, b].astype(F32)
        sb_ref[b] = arrived_rows.astype(BF16)
    rsb_out = []
    for number, b in enumerate(others(b_me, NA)):
        d = copy(sb_ref.at[b], rb_ref.at[b_me], rsb_s.at[number], rsb_r.at[b_me], b_peer(b))
        d.start()
        rsb_out.append(d)

    ua_ref[a_me] = jnp.stack([us_ref[:, blk(a_me, b)] for b in range(NA)], axis=0)
    for a in others(a_me, NA):
        for b in range(NA):
            arrived(ua_ref.at[a, b], ua_r.at[a * NA + b])
    ub_out = []
    number = 0
    for b in others(b_me, NA):
        for a in range(NA):
            d = copy(
                ua_ref.at[a, b],
                ub_ref.at[blk(a, b_me)],
                ub_s.at[number],
                ub_r.at[blk(a, b_me)],
                b_peer(b),
            )
            d.start()
            ub_out.append(d)
            number += 1
    for a in range(NA):
        ub_ref[blk(a, b_me)] = ua_ref[a, b_me]

    wc.wait()
    own_rows = wfull_ref[c].astype(F32) + wrc_ref[...].astype(F32)
    wsa_ref[...] = own_rows.astype(BF16)
    wa_out = []
    for number, a in enumerate(others(a_me, NA)):
        d = copy(wsa_ref.at[a], wra_ref.at[a_me], wa_s.at[number], wa_r.at[a_me], a_peer(a))
        d.start()
        wa_out.append(d)
    wra_ref[a_me] = wsa_ref[a_me]

    total = sb_ref[b_me].astype(F32)
    for b in others(b_me, NA):
        arrived(rb_ref.at[b], rsb_r.at[b])
        total = total + rb_ref[b].astype(F32)
    for g in range(G):
        for jl in range(2):
            sz_ref[g, jl * HC : (jl + 1) * HC, :] = total[:, 2 * g + jl, :]
    rsz_out = []
    for g in others(zc, G):
        d = copy(sz_ref.at[g], rz_ref.at[zc], rsz_s.at[g], rsz_r.at[zc], zc_peer(g))
        d.start()
        rsz_out.append(d)
    rz_ref[zc] = sz_ref[zc]

    for a in others(a_me, NA):
        arrived(wra_ref.at[a], wa_r.at[a])
    wsum = wra_ref[0].astype(F32)
    for a in range(1, NA):
        wsum = wsum + wra_ref[a].astype(F32)
    wrb_ref[b_me] = wsum.astype(BF16)
    wb_out = []
    for number, b in enumerate(others(b_me, NA)):
        d = copy(wrb_ref.at[b_me], wrb_ref.at[b_me], wb_s.at[number], wb_r.at[b_me], b_peer(b))
        d.start()
        wb_out.append(d)

    for b in others(b_me, NA):
        for a in range(NA):
            block = blk(a, b)
            arrived(ub_ref.at[block], ub_r.at[block])
    ux_ref[...] = ub_ref[...].reshape(NB * 2 * BR, C).astype(F32)
    for g in range(G):
        for jl in range(2):
            for r in range(2):
                start = r * BR + 2 * g + jl
                uz_ref[g, jl, r] = ux_ref[pl.ds(start, NB, stride=2 * BR), :].astype(BF16)
    uz_out = []
    for g in others(zc, G):
        d = copy(uz_ref.at[g], ur_ref.at[zc], uz_s.at[g], uz_r.at[zc], zc_peer(g))
        d.start()
        uz_out.append(d)
    ur_ref[zc] = uz_ref[zc]

    d_normed = dot(dproj_ref[...], w_ref[...], NT)

    for b in others(b_me, NA):
        arrived(wrb_ref.at[b], wb_r.at[b])
    wsum = wrb_ref[0].astype(F32)
    for b in range(1, NA):
        wsum = wsum + wrb_ref[b].astype(F32)
    wrz_ref[z] = wsum.astype(BF16)
    wz_out = []
    for number, zz in enumerate(others(z, NZ)):
        d = copy(wrz_ref.at[z], wrz_ref.at[z], wz_s.at[number], wz_r.at[z], z_peer(zz))
        d.start()
        wz_out.append(d)

    for g in others(zc, G):
        arrived(rz_ref.at[g], rsz_r.at[g])
    sums = []
    for core in range(NC):
        part = rz_ref[core]
        for zz in range(1, NZ):
            part = part + rz_ref[zz * NC + core]
        sums.append(part)
    d_bias = []
    for jl in range(2):
        d_bias.append(
            jnp.concatenate([s[jl * HC : (jl + 1) * HC] for s in sums], axis=0)
        )
    d_bias = jnp.concatenate(d_bias, axis=1)
    d_bias = jnp.concatenate([d_bias, jnp.zeros((8 - H, T), F32)], axis=0).astype(BF16)
    small = dot(d_bias, normed_ref[...])
    lane = lax.broadcasted_iota(jnp.int32, (8, C), 1)
    row = lax.broadcasted_iota(jnp.int32, (8, C), 0)
    for h in range(H):
        value = jnp.sum(dbias_ref[h] * same_ref[...], axis=0, keepdims=True)
        value = jnp.sum(value, axis=1, keepdims=True)
        small = jnp.where((row == H) & (lane == h), value, small)

    def exchange(mine, me, n, ref, ssem, rsem, peer):
        ref[me] = mine
        outs = []
        for other in others(me, n):
            d = copy(ref.at[me], ref.at[me], ssem.at[other], rsem.at[me], peer(other))
            d.start()
            outs.append(d)
        return outs

    def collect(me, n, ref, rsem):
        for other in others(me, n):
            arrived(ref.at[other], rsem.at[other])
        out = ref[0]
        for other in range(1, n):
            out = out + ref[other]
        return out

    t0_out = exchange(small, zc, G, t0_ref, t0_s, t0_r, zc_peer)

    bwt = jnp.transpose(bw_ref[...].astype(F32)).astype(BF16)
    d_normed = d_normed + dot(d_bias, bwt, TN)
    standard = std_ref[...]
    mean_grad = jnp.mean(d_normed, axis=-1, keepdims=True)
    mean_cross = jnp.mean(d_normed * standard, axis=-1, keepdims=True)
    pair_grad = (d_normed - mean_grad - standard * mean_cross) * inv_ref[...]
    pg_ref[...] = pair_grad.astype(BF16).reshape(2, N, C)

    small = collect(zc, G, t0_ref, t0_r)
    t1_out = exchange(small, y, NY, t1_ref, t1_s, t1_r, y_peer)

    for zz in others(z, NZ):
        arrived(wrz_ref.at[zz], wz_r.at[zz])
    wsum = wrz_ref[0].astype(F32)
    for zz in range(1, NZ):
        wsum = wsum + wrz_ref[zz].astype(F32)
    wag_ref[c, a_me] = wsum.astype(BF16)
    wga_out = []
    wgc_out = []

    def pass_on(a):
        part = wag_ref.at[c, a]
        d = copy(part, part, wgc_s.at[a], wgc_r.at[a], partner)
        d.start()
        wgc_out.append(d)

    for number, a in enumerate(others(a_me, NA)):
        part = wag_ref.at[c, a_me]
        d = copy(part, part, wga_s.at[number], wga_r.at[a_me], a_peer(a))
        d.start()
        wga_out.append(d)
    pass_on(a_me)

    for g in others(zc, G):
        arrived(ur_ref.at[g], uz_r.at[g])
    for g in range(G):
        for jl in range(2):
            for r in range(2):
                start = jl * N + 2 * g + r
                npt_ref[pl.ds(start, NB, stride=BR), :] = ur_ref[g, jl, r].astype(F32)

    small = collect(y, NY, t1_ref, t1_r)
    t2_out = exchange(small, x, NX, t2_ref, t2_s, t2_r, x_peer)

    for a in others(a_me, NA):
        arrived(wag_ref.at[c, a], wga_r.at[a])
        pass_on(a)
    for a in range(NA):
        arrived(wag_ref.at[1 - c, a], wgc_r.at[a])
    wg_ref[...] = wag_ref[...].reshape(C, 5 * HD).astype(F32) * (1.0 / N)

    small = collect(x, NX, t2_ref, t2_r)
    small_ref[...] = small * (1.0 / N)

    for d in (
        slot_out + ag_out + rsa_out + ua_out + rsb_out + ub_out + wa_out + rsz_out
        + wb_out + uz_out + wz_out + t0_out + t1_out + wga_out + wgc_out + t2_out
    ):
        d.wait_send()
    for t in range(HC):
        rsc(t).wait_send()


def scratch(grid, N):
    NY, NX, NZ, NC = grid
    G, NB, NA, HC = NZ * NC, NX * NY, NX, H // NC
    BR, T, WR = 2 * G, 2 * N, C // NC // NX
    V = pltpu.VMEM
    buffers = [
        V((T, C), F32),
        V((T, C), F32),
        V((T, C), BF16),
        V((T, HD), BF16),
        V((T, HD), BF16),
        V((T, HD), BF16),
        V((T, HD), BF16),
        V((2, HD, N), BF16),
        V((2, HD, N), BF16),
        V((T, HD), F32),
        V((T, HD), F32),
        V((2, N, HD), F32),
        V((2, N, HD), F32),
        V((2, HD, N), F32),
        V((2, HD, N), F32),
        V((N, N), F32),
        V((H, N, N), F32),
        V((T, 4 * HD), BF16),
        V((G, 2 * H, N), BF16),
        V((H, NB, BR, N), BF16),
        V((HC, NB, BR, N), BF16),
        V((HC, NB, BR, N), BF16),
        V((HC, NB, BR, N), BF16),
        V((NA, NA, HC, BR, N), BF16),
        V((NA, HC, BR, N), BF16),
        V((NA, HC, BR, N), BF16),
        V((G, 2 * HC, N), F32),
        V((G, 2 * HC, N), F32),
        V((NA, WR, 5 * HD), BF16),
        V((NA, WR, 5 * HD), BF16),
        V((NA, WR, 5 * HD), BF16),
        V((NA, WR, 5 * HD), BF16),
        V((NA, WR, 5 * HD), BF16),
        V((NZ, WR, 5 * HD), BF16),
        V((NC, NA, WR, 5 * HD), BF16),
        V((2, NB, BR, C), BF16),
        V((NA, NA, 2, BR, C), BF16),
        V((NB, 2, BR, C), BF16),
        V((NB * 2 * BR, C), F32),
        V((G, 2, 2, NB, C), BF16),
        V((G, 2, 2, NB, C), BF16),
        V((G, 8, C), F32),
        V((NY, 8, C), F32),
        V((NX, 8, C), F32),
    ]
    dma = pltpu.SemaphoreType.DMA
    counts = [
        (G, G),
        ((NA - 1) * (NA + 1), NB),
        (NB, NB),
        (HC, HC),
        ((NA - 1) * NA, NB),
        (NA - 1, NA),
        (G, G),
        (None, None),
        (NA - 1, NA),
        (NA - 1, NA),
        (NZ - 1, NZ),
        (NA - 1, NA),
        (NA, NA),
        ((NA - 1) * NA, NB),
        ((NA - 1) * NA, NB),
        (G, G),
        (G, G),
        (NY, NY),
        (NX, NX),
    ]
    for pair in counts:
        for n in pair:
            buffers.append(dma if n is None else dma((n,)))
    return buffers


def body(
    grid, pair, token_mask, chain_ids, proj_weight, bias_weight, chain_weight, out_weight, cotangent
):
    N = pair.shape[1]
    vmem = pl.BlockSpec(memory_space=pltpu.VMEM)
    smem = pl.BlockSpec(memory_space=pltpu.SMEM)
    bias_padded = jnp.pad(bias_weight, ((0, 0), (0, 8 - H)))
    npt, pair_grad, weights, small = pl.pallas_call(
        functools.partial(kernel, grid, N),
        out_shape=(
            jax.ShapeDtypeStruct((2 * N, C), F32),
            jax.ShapeDtypeStruct((2, N, C), BF16),
            jax.ShapeDtypeStruct((C, 5 * HD), F32),
            jax.ShapeDtypeStruct((8, C), F32),
        ),
        in_specs=[smem] + [vmem] * 7,
        out_specs=(vmem,) * 4,
        scratch_shapes=scratch(grid, N),
        compiler_params=pltpu.CompilerParams(collective_id=0, has_side_effects=True),
    )(
        chain_weight,
        pair,
        token_mask.reshape(1, N),
        chain_ids.reshape(1, N),
        proj_weight,
        bias_padded,
        out_weight,
        cotangent,
    )
    return (
        npt.reshape(2, N, C),
        pair_grad,
        weights[:, 0 : 4 * HD],
        jnp.transpose(small[0:H, :]),
        small[H, 0:H],
        weights[:, 4 * HD :],
    )


def solution(mesh, grid=GRID):
    return jax.shard_map(
        functools.partial(body, grid),
        mesh=mesh,
        in_specs=(
            P(("dp", "dap"), None, None),
            P("dp"),
            P("dp"),
            P(),
            P(),
            P(),
            P(),
            P(("dp", "dap"), None, None),
        ),
        out_specs=(
            P(("dp", "dap"), None, None),
            P(("dp", "dap"), None, None),
            P("dp", None),
            P("dp", None),
            P("dp"),
            P("dp", None),
        ),
        check_vma=False,
    )
```

```python
import functools

import jax
import jax.numpy as jnp
from jax import lax
from jax.experimental import pallas as pl
from jax.experimental.pallas import tpu as pltpu
from jax.sharding import PartitionSpec as P

H = 4
DH = 32
HD = 128
C = 128
GRID = (4, 4, 4, 2)
EPSILON = 1e-05

F32 = jnp.float32
BF16 = jnp.bfloat16
NN = (((1,), (0,)), ((), ()))
NT = (((1,), (1,)), ((), ()))
TN = (((0,), (0,)), ((), ()))


def dot(a, b, dims=NN):
    return lax.dot_general(a, b, dims, preferred_element_type=F32)


def kernel(
    grid,
    tokens,
    cw_hbm,
    pair_hbm,
    mask_hbm,
    chain_hbm,
    w_hbm,
    bw_hbm,
    ow_hbm,
    cot_hbm,
    npt_o,
    pg_o,
    wag_o,
    small_o,
    cw_ref,
    pair_ref,
    mask_ref,
    chain_ref,
    w_ref,
    bw_ref,
    ow_ref,
    cot_ref,
    npt_ref,
    pg_ref,
    small_ref,
    std_ref,
    inv_ref,
    normed_ref,
    q_ref,
    k_ref,
    v_ref,
    da_ref,
    qt_ref,
    dat_ref,
    gate_ref,
    dgated_ref,
    att_ref,
    dq_ref,
    dkt_ref,
    dvt_ref,
    same_ref,
    dbias_ref,
    dproj_ref,
    s0_ref,
    dp_ref,
    slot_ref,
    bias_ref,
    sc_ref,
    rc_ref,
    sa_ref,
    ra_ref,
    sz_ref,
    rz_ref,
    wfull_ref,
    wrc_ref,
    wsa_ref,
    wra_ref,
    wrz_ref,
    wag_ref,
    us_ref,
    ub_ref,
    ux_ref,
    uz_ref,
    ur_ref,
    t0_ref,
    t1_ref,
    in_s,
    out_s,
    slot_s,
    slot_r,
    ag_s,
    ag_r,
    agc_s,
    agc_r,
    rsc_s,
    rsc_r,
    rsa_s,
    rsa_r,
    rsz_s,
    rsz_r,
    wc_s,
    wc_r,
    wa_s,
    wa_r,
    wz_s,
    wz_r,
    wga_s,
    wga_r,
    wgc_s,
    wgc_r,
    ua_s,
    ua_r,
    uz_s,
    uz_r,
    t0_s,
    t0_r,
    t1_s,
    t1_r,
):
    NY, NX, NZ, NC = grid
    G = NZ * NC
    NB = NX * NY
    BR = 2 * G
    N = tokens
    T = 2 * N
    HC = H // NC

    idx = lax.axis_index("dap")
    zc = lax.rem(idx, G)
    c = lax.rem(idx, NC)
    z = lax.div(zc, NC)
    yx = lax.div(idx, G)
    x = lax.rem(yx, NX)
    y = lax.div(yx, NX)
    partner = idx + 1 - 2 * c
    far = HC * (1 - c)
    near = HC * c

    def zc_peer(g):
        return idx + g - zc

    def yx_peer(b):
        return idx + (b - yx) * G

    def z_peer(zz):
        return idx + (zz - z) * NC

    def others(me, n):
        return [lax.rem(me + d, n) for d in range(1, n)]

    steps = [(i, j) for i in range(NY) for j in range(NX) if i or j]
    steps.sort(key=lambda s: -min(s[0], NY - s[0]) - min(s[1], NX - s[1]))
    plane = [lax.rem(y + i, NY) * NX + lax.rem(x + j, NX) for i, j in steps]
    column = others(zc, G)

    def copy(src, dst, ssem, rsem, dev):
        return pltpu.make_async_remote_copy(
            src_ref=src,
            dst_ref=dst,
            send_sem=ssem,
            recv_sem=rsem,
            device_id={"dap": dev},
            device_id_type=pl.DeviceIdType.MESH,
        )

    sent = []

    def send(src, dst, ssem, rsem, dev):
        d = copy(src, dst, ssem, rsem, dev)
        d.start()
        sent.append(d)

    def arrived(ref, sem):
        copy(ref, ref, sem, sem, partner).wait_recv()

    barrier = pltpu.get_barrier_semaphore()
    peers = [yx_peer(b) for b in plane] + [zc_peer(g) for g in column]
    for p in peers:
        pl.semaphore_signal(
            barrier, inc=1, device_id={"dap": p}, device_id_type=pl.DeviceIdType.MESH
        )

    loads = []
    for number, (src, dst) in enumerate(
        (
            (pair_hbm, pair_ref),
            (bw_hbm, bw_ref),
            (w_hbm, w_ref),
            (cot_hbm, cot_ref),
            (ow_hbm, ow_ref),
            (chain_hbm, chain_ref),
            (mask_hbm, mask_ref),
            (cw_hbm, cw_ref),
        )
    ):
        d = pltpu.make_async_copy(src, dst, in_s.at[number])
        d.start()
        loads.append(d)
    loads[0].wait()

    values = pair_ref[...].reshape(T, C).astype(F32)
    centered = values - jnp.mean(values, axis=-1, keepdims=True)
    inverse = lax.rsqrt(jnp.mean(centered * centered, axis=-1, keepdims=True) + EPSILON)
    standard = centered * inverse
    std_ref[...] = standard
    inv_ref[...] = jnp.broadcast_to(inverse, (T, C))
    normed = standard.astype(BF16)
    normed_ref[...] = normed
    loads[1].wait()
    bwt = jnp.concatenate([bw_ref[...].astype(F32), jnp.zeros((8 - H, C), F32)], axis=0)
    bwt = bwt.astype(BF16)
    local_bias = dot(bwt, normed, NT)
    slot_ref[zc] = jnp.concatenate(
        [local_bias[0:H, 0:N], local_bias[0:H, N:T]], axis=0
    ).astype(BF16)

    pl.semaphore_wait(barrier, len(peers))
    for g in column:
        send(slot_ref.at[zc], slot_ref.at[zc], slot_s.at[g], slot_r.at[zc], zc_peer(g))

    for d in loads[2:]:
        d.wait()
    projected = dot(normed, w_ref[...])
    scaling = DH ** (-0.5)
    q32 = projected[:, 0:HD] * scaling
    q_ref[...] = q32.astype(BF16)
    k_ref[...] = projected[:, HD : 2 * HD].astype(BF16)
    v_ref[...] = projected[:, 2 * HD : 3 * HD].astype(BF16)
    gating = jax.nn.sigmoid(projected[:, 3 * HD :])
    gate_ref[...] = gating
    d_gated = dot(cot_ref[...].reshape(T, C), ow_ref[...], NT)
    dgated_ref[...] = d_gated
    da32 = d_gated * gating
    da_ref[...] = da32.astype(BF16)
    for r in range(2):
        rows = slice(r * N, (r + 1) * N)
        qt_ref[r] = jnp.transpose(q32[rows]).astype(BF16)
        dat_ref[r] = jnp.transpose(da32[rows]).astype(BF16)

    for g in column:
        arrived(slot_ref.at[g], slot_r.at[g])
    gathered = slot_ref[...].reshape(G * 2 * H, N)
    for t in range(HC):
        at = lax.broadcasted_iota(jnp.int32, (BR, G * 2 * H), 0) * H + (far + t)
        pick = (at == lax.broadcasted_iota(jnp.int32, (BR, G * 2 * H), 1)).astype(BF16)
        bias_ref[far + t, yx] = dot(pick, gathered).astype(BF16)

    def bias_block(first, block):
        return bias_ref.at[pl.ds(first, HC), block]

    def hand_over(block):
        part = bias_block(far, block)
        send(part, part, agc_s.at[block], agc_r.at[block], partner)

    for number, b in enumerate(plane):
        part = bias_block(far, yx)
        send(part, part, ag_s.at[number], ag_r.at[yx], yx_peer(b))
    hand_over(yx)

    chain = chain_ref[...].astype(F32)
    chain_cols = jnp.transpose(jnp.broadcast_to(chain, (HD, N)))
    chain_cols = jnp.concatenate([chain_cols] * (-(-N // HD)), axis=1)[:, 0:N]
    same_ref[...] = (chain_cols == jnp.broadcast_to(chain, (N, N))).astype(F32)
    masked = (mask_ref[...].astype(F32) - 1.0) * 1000000000.0
    head_of = lax.broadcasted_iota(jnp.int32, (N, HD), 1) // DH
    none = jnp.zeros((N, HD), BF16)

    @pl.loop(0, H)
    def _(h):
        own = head_of == h
        lane = lax.broadcasted_iota(jnp.int32, (1, H), 1) == h
        weight = jnp.sum(jnp.where(lane, cw_ref[...], 0.0), axis=1, keepdims=True)
        extra = weight * same_ref[...] + masked
        for r in range(2):
            rows = slice(r * N, (r + 1) * N)
            products = dot(jnp.where(own, q_ref[rows, :], none), k_ref[rows, :], NT)
            s0_ref[r, h] = products + extra
            dp_ref[r, h] = dot(jnp.where(own, da_ref[rows, :], none), v_ref[rows, :], NT)

    for b in plane:
        arrived(bias_block(far, b), ag_r.at[b])
        hand_over(b)

    att_ref[...] = jnp.zeros((2, N, HD), F32)
    dq_ref[...] = jnp.zeros((2, N, HD), F32)

    def one_head(h):
        own = head_of == h
        bias = bias_ref[h].reshape(N, N).astype(F32)
        head_rows = pl.ds(pl.multiple_of(h * DH, DH), DH)
        for r in range(2):
            rows = slice(r * N, (r + 1) * N)
            scores = s0_ref[r, h] + bias
            expo = jnp.exp(scores - jnp.max(scores, axis=1, keepdims=True))
            probs = expo * (1.0 / jnp.sum(expo, axis=1, keepdims=True))
            probs_low = probs.astype(BF16)
            att_ref[r] += dot(probs_low, jnp.where(own, v_ref[rows, :], none))
            d_probs = dp_ref[r, h]
            inner = jnp.sum(probs * d_probs, axis=1, keepdims=True)
            d_scores = probs * (d_probs - inner)
            low = d_scores.astype(BF16)
            dq_ref[r] += dot(low, jnp.where(own, k_ref[rows, :], none))
            dkt_ref[r, head_rows, :] = dot(qt_ref[r, head_rows, :], low)
            dvt_ref[r, head_rows, :] = dot(dat_ref[r, head_rows, :], probs_low)
            if r == 0:
                dbias_ref[h] = d_scores
            else:
                dbias_ref[h] += d_scores

    def rsc(t):
        return copy(sc_ref.at[t], rc_ref.at[t], rsc_s.at[t], rsc_r.at[t], partner)

    @pl.loop(0, HC)
    def _(t):
        one_head(far + t)
        sc_ref[t] = dbias_ref[far + t].reshape(NB, BR, N).astype(BF16)
        rsc(t).start()

    for b in [yx] + plane:
        arrived(bias_block(near, b), agc_r.at[b])

    def plane_copy(t, number):
        b = plane[number]
        return copy(
            sa_ref.at[t, b],
            ra_ref.at[yx, t],
            rsa_s.at[t, number],
            rsa_r.at[t, yx],
            yx_peer(b),
        )

    @pl.loop(0, HC)
    def _(t):
        one_head(near + t)
        rsc(t).wait_recv()
        total = dbias_ref[near + t] + rc_ref[t].reshape(N, N).astype(F32)
        sa_ref[t] = total.reshape(NB, BR, N).astype(BF16)
        for number in range(NB - 1):
            plane_copy(t, number).start()

    attended = att_ref[...].reshape(T, HD)
    gating = gate_ref[...]
    gated = (gating * attended).astype(BF16)
    update = dot(gated, ow_ref[...])
    next_pair = pair_ref[...].reshape(T, C).astype(F32) + update
    us_ref[...] = next_pair.astype(BF16).reshape(2, NB, BR, C)
    for number, b in enumerate(plane):
        send(us_ref.at[:, b], ub_ref.at[yx], ua_s.at[number], ua_r.at[yx], yx_peer(b))
    ub_ref[yx] = us_ref[:, yx]

    d_gate = dgated_ref[...] * attended * gating * (1.0 - gating)
    dproj_ref[:, 0:HD] = (dq_ref[...].reshape(T, HD) * scaling).astype(BF16)
    for r in range(2):
        rows = slice(r * N, (r + 1) * N)
        dproj_ref[rows, HD : 2 * HD] = jnp.transpose(dkt_ref[r]).astype(BF16)
        dproj_ref[rows, 2 * HD : 3 * HD] = jnp.transpose(dvt_ref[r]).astype(BF16)
    dproj_ref[:, 3 * HD :] = d_gate.astype(BF16)
    proj_part = dot(normed_ref[...], dproj_ref[...], TN)
    out_part = dot(gated, cot_ref[...].reshape(T, C), TN)
    wfull_ref[0] = proj_part[:, 0 : 3 * HD].reshape(16, 8, 3 * HD).astype(BF16)
    wfull_ref[1, :, :, 0:HD] = proj_part[:, 3 * HD :].reshape(16, 8, HD).astype(BF16)
    wfull_ref[1, :, :, HD : 2 * HD] = out_part.reshape(16, 8, HD).astype(BF16)
    wfull_ref[1, :, :, 2 * HD :] = jnp.zeros((16, 8, HD), BF16)
    wc = copy(wfull_ref.at[1 - c], wrc_ref, wc_s, wc_r, partner)
    wc.start()

    chain_sums = jnp.zeros((8, C), F32)
    lane = lax.broadcasted_iota(jnp.int32, (8, C), 1)
    row = lax.broadcasted_iota(jnp.int32, (8, C), 0)
    for h in range(H):
        value = jnp.sum(dbias_ref[h] * same_ref[...], axis=0, keepdims=True)
        value = jnp.sum(value, axis=1, keepdims=True)
        chain_sums = jnp.where((row == H) & (lane == h), value, chain_sums)

    total = sa_ref[:, yx].astype(F32)
    for b in plane:
        for t in range(HC):
            arrived(ra_ref.at[b, t], rsa_r.at[t, b])
        total = total + ra_ref[b].astype(F32)
    for g in range(G):
        for jl in range(2):
            sz_ref[g, jl * HC : (jl + 1) * HC, :] = total[:, 2 * g + jl, :]
    for g in column:
        send(sz_ref.at[g], rz_ref.at[zc], rsz_s.at[g], rsz_r.at[zc], zc_peer(g))
    rz_ref[zc] = sz_ref[zc]

    wc.wait()
    own_half = wfull_ref[c].astype(F32) + wrc_ref[...].astype(F32)
    wsa_ref[...] = own_half.reshape(NB, 128 // NB, 3 * HD).astype(BF16)
    for number, b in enumerate(plane):
        send(wsa_ref.at[b], wra_ref.at[yx], wa_s.at[number], wa_r.at[yx], yx_peer(b))
    wra_ref[yx] = wsa_ref[yx]

    for b in plane:
        arrived(ub_ref.at[b], ua_r.at[b])
    ux_ref[...] = ub_ref[...].reshape(NB * 2 * BR, C).astype(F32)
    for g in range(G):
        for jl in range(2):
            for r in range(2):
                start = r * BR + 2 * g + jl
                uz_ref[g, jl, r] = ux_ref[pl.ds(start, NB, stride=2 * BR), :].astype(BF16)
    for g in column:
        send(uz_ref.at[g], ur_ref.at[zc], uz_s.at[g], uz_r.at[zc], zc_peer(g))
    ur_ref[zc] = uz_ref[zc]

    d_normed = dot(dproj_ref[...], w_ref[...], NT)

    for b in plane:
        arrived(wra_ref.at[b], wa_r.at[b])
    wsum = wra_ref[0].astype(F32)
    for b in range(1, NB):
        wsum = wsum + wra_ref[b].astype(F32)
    wrz_ref[z] = wsum.astype(BF16)
    for number, zz in enumerate(others(z, NZ)):
        send(wrz_ref.at[z], wrz_ref.at[z], wz_s.at[number], wz_r.at[z], z_peer(zz))

    for g in column:
        arrived(rz_ref.at[g], rsz_r.at[g])
    sums = []
    for core in range(NC):
        part = rz_ref[core]
        for zz in range(1, NZ):
            part = part + rz_ref[zz * NC + core]
        sums.append(part)
    d_bias = []
    for jl in range(2):
        d_bias.append(
            jnp.concatenate([s[jl * HC : (jl + 1) * HC] for s in sums], axis=0)
        )
    d_bias = jnp.concatenate(d_bias, axis=1)
    d_bias = jnp.concatenate([d_bias, jnp.zeros((8 - H, T), F32)], axis=0).astype(BF16)

    t0_ref[zc] = dot(d_bias, normed_ref[...]) + chain_sums
    for g in column:
        send(t0_ref.at[zc], t0_ref.at[zc], t0_s.at[g], t0_r.at[zc], zc_peer(g))

    d_normed = d_normed + dot(d_bias, bwt, TN)
    standard = std_ref[...]
    mean_grad = jnp.mean(d_normed, axis=-1, keepdims=True)
    mean_cross = jnp.mean(d_normed * standard, axis=-1, keepdims=True)
    pair_grad = (d_normed - mean_grad - standard * mean_cross) * inv_ref[...]
    pg_ref[...] = pair_grad.astype(BF16)
    pg_out = pltpu.make_async_copy(pg_ref, pg_o, out_s.at[0])
    pg_out.start()

    for g in column:
        arrived(ur_ref.at[g], uz_r.at[g])
    for g in range(G):
        for jl in range(2):
            for r in range(2):
                start = jl * N + 2 * g + r
                npt_ref[pl.ds(start, NB, stride=BR), :] = ur_ref[g, jl, r].astype(F32)
    npt_out = pltpu.make_async_copy(npt_ref, npt_o, out_s.at[1])
    npt_out.start()

    for zz in others(z, NZ):
        arrived(wrz_ref.at[zz], wz_r.at[zz])
    wsum = wrz_ref[0].astype(F32)
    for zz in range(1, NZ):
        wsum = wsum + wrz_ref[zz].astype(F32)
    wag_ref[c, yx] = wsum.astype(BF16)

    def pass_on(b):
        part = wag_ref.at[c, b]
        send(part, part, wgc_s.at[b], wgc_r.at[b], partner)

    for number, b in enumerate(plane):
        part = wag_ref.at[c, yx]
        send(part, part, wga_s.at[number], wga_r.at[yx], yx_peer(b))
    pass_on(yx)

    for g in column:
        arrived(t0_ref.at[g], t0_r.at[g])
    small = t0_ref[0]
    for g in range(1, G):
        small = small + t0_ref[g]
    t1_ref[yx] = small
    for number, b in enumerate(plane):
        send(t1_ref.at[yx], t1_ref.at[yx], t1_s.at[number], t1_r.at[yx], yx_peer(b))

    for b in plane:
        arrived(wag_ref.at[c, b], wga_r.at[b])
        pass_on(b)
    for b in [yx] + plane:
        arrived(wag_ref.at[1 - c, b], wgc_r.at[b])
    wag_out = pltpu.make_async_copy(wag_ref, wag_o, out_s.at[2])
    wag_out.start()

    for b in plane:
        arrived(t1_ref.at[b], t1_r.at[b])
    small = t1_ref[0]
    for b in range(1, NB):
        small = small + t1_ref[b]
    small_ref[...] = small * (1.0 / N)
    small_out = pltpu.make_async_copy(small_ref, small_o, out_s.at[3])
    small_out.start()

    for d in sent:
        d.wait_send()
    for t in range(HC):
        rsc(t).wait_send()
        for number in range(NB - 1):
            plane_copy(t, number).wait_send()
    for d in (pg_out, npt_out, wag_out, small_out):
        d.wait()


def scratch(grid, N):
    NY, NX, NZ, NC = grid
    G, NB, HC = NZ * NC, NX * NY, H // NC
    BR, T, WR = 2 * G, 2 * N, 128 // NB
    V = pltpu.VMEM
    buffers = [
        V((1, H), F32),
        V((2, N, C), BF16),
        V((1, N), jnp.int32),
        V((1, N), jnp.int32),
        V((C, 4 * HD), BF16),
        V((H, C), BF16),
        V((HD, C), BF16),
        V((2, N, C), BF16),
        V((T, C), F32),
        V((T, C), BF16),
        V((8, C), F32),
        V((T, C), F32),
        V((T, C), F32),
        V((T, C), BF16),
        V((T, HD), BF16),
        V((T, HD), BF16),
        V((T, HD), BF16),
        V((T, HD), BF16),
        V((2, HD, N), BF16),
        V((2, HD, N), BF16),
        V((T, HD), F32),
        V((T, HD), F32),
        V((2, N, HD), F32),
        V((2, N, HD), F32),
        V((2, HD, N), F32),
        V((2, HD, N), F32),
        V((N, N), F32),
        V((H, N, N), F32),
        V((T, 4 * HD), BF16),
        V((2, H, N, N), F32),
        V((2, H, N, N), F32),
        V((G, 2 * H, N), BF16),
        V((H, NB, BR, N), BF16),
        V((HC, NB, BR, N), BF16),
        V((HC, NB, BR, N), BF16),
        V((HC, NB, BR, N), BF16),
        V((NB, HC, BR, N), BF16),
        V((G, 2 * HC, N), F32),
        V((G, 2 * HC, N), F32),
        V((NC, 16, 8, 3 * HD), BF16),
        V((16, 8, 3 * HD), BF16),
        V((NB, WR, 3 * HD), BF16),
        V((NB, WR, 3 * HD), BF16),
        V((NZ, WR, 3 * HD), BF16),
        V((NC, NB, WR, 3 * HD), BF16),
        V((2, NB, BR, C), BF16),
        V((NB, 2, BR, C), BF16),
        V((NB * 2 * BR, C), F32),
        V((G, 2, 2, NB, C), BF16),
        V((G, 2, 2, NB, C), BF16),
        V((G, 8, C), F32),
        V((NB, 8, C), F32),
    ]
    dma = pltpu.SemaphoreType.DMA
    counts = [
        ((8,), (4,)),
        ((G,), (G,)),
        ((NB,), (NB,)),
        ((NB,), (NB,)),
        ((HC,), (HC,)),
        ((HC, NB), (HC, NB)),
        ((G,), (G,)),
        (None, None),
        ((NB,), (NB,)),
        ((NZ,), (NZ,)),
        ((NB,), (NB,)),
        ((NB,), (NB,)),
        ((NB,), (NB,)),
        ((G,), (G,)),
        ((G,), (G,)),
        ((NB,), (NB,)),
    ]
    for both in counts:
        for shape in both:
            buffers.append(dma if shape is None else dma(shape))
    return buffers


def finish(npt_ref, pg_ref, wag_ref, small_ref, npt_o, pg_o, wg_o, bg_o, cg_o, og_o):
    N = npt_o.shape[1]
    npt_o[...] = npt_ref[...].reshape(2, N, C)
    pg_o[...] = pg_ref[...].reshape(2, N, C)
    scale = 1.0 / N
    first = wag_ref[0].astype(F32).reshape(C, 3 * HD) * scale
    second = wag_ref[1].astype(F32).reshape(C, 3 * HD) * scale
    wg_o[:, 0 : 3 * HD] = first
    wg_o[:, 3 * HD :] = second[:, 0:HD]
    og_o[...] = second[:, HD : 2 * HD]
    bg_o[...] = small_ref[0:H, :]
    cg_o[...] = small_ref[H : H + 1, 0:H]


def body(
    grid, pair, token_mask, chain_ids, proj_weight, bias_weight, chain_weight, out_weight, cotangent
):
    N = pair.shape[1]
    NY, NX, NZ, NC = grid
    vmem = pl.BlockSpec(memory_space=pltpu.VMEM)
    hbm = pl.BlockSpec(memory_space=pl.ANY)
    results = pl.pallas_call(
        functools.partial(kernel, grid, N),
        out_shape=(
            jax.ShapeDtypeStruct((2 * N, C), F32),
            jax.ShapeDtypeStruct((2 * N, C), BF16),
            jax.ShapeDtypeStruct((NC, NX * NY, 128 // (NX * NY), 3 * HD), BF16),
            jax.ShapeDtypeStruct((8, C), F32),
        ),
        in_specs=[hbm] * 8,
        out_specs=(hbm,) * 4,
        scratch_shapes=scratch(grid, N),
        compiler_params=pltpu.CompilerParams(collective_id=0, has_side_effects=True),
    )(
        chain_weight.reshape(1, H),
        pair,
        token_mask.reshape(1, N),
        chain_ids.reshape(1, N),
        proj_weight,
        jnp.transpose(bias_weight),
        out_weight,
        cotangent,
    )
    npt, pair_grad, weight_grad, bias_grad, chain_grad, out_grad = pl.pallas_call(
        finish,
        out_shape=(
            jax.ShapeDtypeStruct((2, N, C), F32),
            jax.ShapeDtypeStruct((2, N, C), BF16),
            jax.ShapeDtypeStruct((C, 4 * HD), F32),
            jax.ShapeDtypeStruct((H, C), F32),
            jax.ShapeDtypeStruct((1, H), F32),
            jax.ShapeDtypeStruct((HD, C), F32),
        ),
        in_specs=[vmem] * 4,
        out_specs=(vmem,) * 6,
    )(*results)
    return (
        npt,
        pair_grad,
        weight_grad,
        jnp.transpose(bias_grad),
        chain_grad.reshape(H),
        out_grad,
    )


def solution(mesh, grid=GRID):
    return jax.shard_map(
        functools.partial(body, grid),
        mesh=mesh,
        in_specs=(
            P(("dp", "dap"), None, None),
            P("dp"),
            P("dp"),
            P(),
            P(),
            P(),
            P(),
            P(("dp", "dap"), None, None),
        ),
        out_specs=(
            P(("dp", "dap"), None, None),
            P(("dp", "dap"), None, None),
            P("dp", None),
            P("dp", None),
            P("dp"),
            P("dp", None),
        ),
        check_vma=False,
    )
```

```python
import functools

import jax
import jax.numpy as jnp
from jax import lax
from jax.experimental import pallas as pl
from jax.experimental.pallas import tpu as pltpu
from jax.sharding import PartitionSpec as P

H = 4
DH = 32
HD = 128
C = 128
GRID = (4, 4, 4, 2)
EPSILON = 1e-05

F32 = jnp.float32
BF16 = jnp.bfloat16
NN = (((1,), (0,)), ((), ()))
NT = (((1,), (1,)), ((), ()))
TN = (((0,), (0,)), ((), ()))


def dot(a, b, dims=NN):
    return lax.dot_general(a, b, dims, preferred_element_type=F32)


def kernel(
    grid,
    tokens,
    cw_hbm,
    pair_hbm,
    mask_hbm,
    chain_hbm,
    w_hbm,
    bw_hbm,
    ow_hbm,
    cot_hbm,
    npt_o,
    pg_o,
    wag_o,
    small_o,
    cw_ref,
    pair_ref,
    mask_ref,
    chain_ref,
    w_ref,
    bw_ref,
    ow_ref,
    cot_ref,
    std_ref,
    inv_ref,
    normed_ref,
    q_ref,
    k_ref,
    v_ref,
    da_ref,
    qt_ref,
    dat_ref,
    gate_ref,
    dgated_ref,
    att_ref,
    dq_ref,
    dkt_ref,
    dvt_ref,
    same_ref,
    dbias_ref,
    dproj_ref,
    s0_ref,
    dp_ref,
    slot_ref,
    bias_ref,
    sc_ref,
    rc_ref,
    sa_ref,
    ra_ref,
    sz_ref,
    rz_ref,
    wfull_ref,
    wrc_ref,
    wsa_ref,
    wra_ref,
    wrz_ref,
    wag_ref,
    us_ref,
    ub_ref,
    ux_ref,
    uz_ref,
    ur_ref,
    t0_ref,
    t1_ref,
    in_s,
    slot_s,
    slot_r,
    ag_s,
    ag_r,
    agc_s,
    agc_r,
    rsc_s,
    rsc_r,
    rsa_s,
    rsa_r,
    rsz_s,
    rsz_r,
    wc_s,
    wc_r,
    wa_s,
    wa_r,
    wz_s,
    wz_r,
    wga_s,
    wga_r,
    wgc_s,
    wgc_r,
    ua_s,
    ua_r,
    uz_s,
    uz_r,
    t0_s,
    t0_r,
    t1_s,
    t1_r,
):
    NY, NX, NZ, NC = grid
    G = NZ * NC
    NB = NX * NY
    BR = 2 * G
    N = tokens
    T = 2 * N
    HC = H // NC

    idx = lax.axis_index("dap")
    zc = lax.rem(idx, G)
    c = lax.rem(idx, NC)
    z = lax.div(zc, NC)
    yx = lax.div(idx, G)
    x = lax.rem(yx, NX)
    y = lax.div(yx, NX)
    partner = idx + 1 - 2 * c
    far = HC * (1 - c)
    near = HC * c

    def zc_peer(g):
        return idx + g - zc

    def yx_peer(b):
        return idx + (b - yx) * G

    def z_peer(zz):
        return idx + (zz - z) * NC

    def others(me, n):
        return [lax.rem(me + d, n) for d in range(1, n)]

    steps = [(i, j) for i in range(NY) for j in range(NX) if i or j]
    steps.sort(key=lambda s: -min(s[0], NY - s[0]) - min(s[1], NX - s[1]))
    plane = [lax.rem(y + i, NY) * NX + lax.rem(x + j, NX) for i, j in steps]
    reach = list(range(1, G))
    reach.sort(key=lambda d: -min(d // NC, NZ - d // NC))
    column = [lax.rem(zc - c + d - d % NC, G) + lax.rem(c + d, NC) for d in reach]

    def copy(src, dst, ssem, rsem, dev):
        return pltpu.make_async_remote_copy(
            src_ref=src,
            dst_ref=dst,
            send_sem=ssem,
            recv_sem=rsem,
            device_id={"dap": dev},
            device_id_type=pl.DeviceIdType.MESH,
        )

    drains = []

    def send(src, dst, ssem, rsem, dev):
        copy(src, dst, ssem, rsem, dev).start()

    def arrived(ref, sem):
        copy(ref, ref, sem, sem, partner).wait_recv()

    def later(ref, sem):
        drains.append(copy(ref, ref, sem, sem, partner))

    barrier = pltpu.get_barrier_semaphore()
    peers = [zc_peer(g) for g in column] + [yx_peer(b) for b in plane]
    for p in peers:
        pl.semaphore_signal(
            barrier, inc=1, device_id={"dap": p}, device_id_type=pl.DeviceIdType.MESH
        )

    loads = []
    for number, (src, dst) in enumerate(
        (
            (pair_hbm, pair_ref),
            (bw_hbm, bw_ref),
            (w_hbm, w_ref),
            (cot_hbm, cot_ref),
            (ow_hbm, ow_ref),
            (chain_hbm, chain_ref),
            (mask_hbm, mask_ref),
            (cw_hbm, cw_ref),
        )
    ):
        d = pltpu.make_async_copy(src, dst, in_s.at[number])
        d.start()
        loads.append(d)
    loads[0].wait()

    values = pair_ref[...].reshape(T, C).astype(F32)
    centered = values - jnp.mean(values, axis=-1, keepdims=True)
    inverse = lax.rsqrt(jnp.mean(centered * centered, axis=-1, keepdims=True) + EPSILON)
    standard = centered * inverse
    std_ref[...] = standard
    inv_ref[...] = jnp.broadcast_to(inverse, (T, C))
    normed = standard.astype(BF16)
    normed_ref[...] = normed
    loads[1].wait()
    bwt = jnp.concatenate([bw_ref[...].astype(F32), jnp.zeros((8 - H, C), F32)], axis=0)
    bwt = bwt.astype(BF16)
    local_bias = dot(bwt, normed, NT)
    slot_ref[zc] = jnp.concatenate(
        [local_bias[0:H, 0:N], local_bias[0:H, N:T]], axis=0
    ).astype(BF16)

    pl.semaphore_wait(barrier, len(peers))
    for g in column:
        send(slot_ref.at[zc], slot_ref.at[zc], slot_s, slot_r, zc_peer(g))
    later(slot_ref.at[pl.ds(0, G - 1)], slot_s)

    for d in loads[2:]:
        d.wait()
    projected = dot(normed, w_ref[...])
    scaling = DH ** (-0.5)
    q32 = projected[:, 0:HD] * scaling
    q_ref[...] = q32.astype(BF16)
    k_ref[...] = projected[:, HD : 2 * HD].astype(BF16)
    v_ref[...] = projected[:, 2 * HD : 3 * HD].astype(BF16)
    gating = jax.nn.sigmoid(projected[:, 3 * HD :])
    gate_ref[...] = gating
    d_gated = dot(cot_ref[...].reshape(T, C), ow_ref[...], NT)
    dgated_ref[...] = d_gated
    da32 = d_gated * gating
    da_ref[...] = da32.astype(BF16)
    for r in range(2):
        rows = slice(r * N, (r + 1) * N)
        qt_ref[r] = jnp.transpose(q32[rows]).astype(BF16)
        dat_ref[r] = jnp.transpose(da32[rows]).astype(BF16)

    arrived(slot_ref.at[pl.ds(0, G - 1)], slot_r)
    gathered = slot_ref[...].reshape(G * 2 * H, N)
    for t in range(HC):
        at = lax.broadcasted_iota(jnp.int32, (BR, G * 2 * H), 0) * H + (far + t)
        pick = (at == lax.broadcasted_iota(jnp.int32, (BR, G * 2 * H), 1)).astype(BF16)
        bias_ref[far + t, yx] = dot(pick, gathered).astype(BF16)

    part = bias_ref.at[pl.ds(far, HC), yx]
    for b in plane:
        send(part, part, ag_s, ag_r, yx_peer(b))
    most = bias_ref.at[pl.ds(far, HC), pl.ds(0, NB - 1)]
    later(most, ag_s)

    chain = chain_ref[...].astype(F32)
    chain_cols = jnp.transpose(jnp.broadcast_to(chain, (HD, N)))
    chain_cols = jnp.concatenate([chain_cols] * (-(-N // HD)), axis=1)[:, 0:N]
    same_ref[...] = (chain_cols == jnp.broadcast_to(chain, (N, N))).astype(F32)
    masked = (mask_ref[...].astype(F32) - 1.0) * 1000000000.0
    head_of = lax.broadcasted_iota(jnp.int32, (N, HD), 1) // DH
    none = jnp.zeros((N, HD), BF16)

    @pl.loop(0, H)
    def _(h):
        own = head_of == h
        lane = lax.broadcasted_iota(jnp.int32, (1, H), 1) == h
        weight = jnp.sum(jnp.where(lane, cw_ref[...], 0.0), axis=1, keepdims=True)
        extra = weight * same_ref[...] + masked
        for r in range(2):
            rows = slice(r * N, (r + 1) * N)
            products = dot(jnp.where(own, q_ref[rows, :], none), k_ref[rows, :], NT)
            s0_ref[r, h] = products + extra
            dp_ref[r, h] = dot(jnp.where(own, da_ref[rows, :], none), v_ref[rows, :], NT)

    arrived(most, ag_r)

    def handed(first, t):
        part = bias_ref.at[first + t]
        return copy(part, part, agc_s.at[t], agc_r.at[t], partner)

    for t in range(HC):
        handed(far, t).start()

    att_ref[...] = jnp.zeros((2, N, HD), F32)
    dq_ref[...] = jnp.zeros((2, N, HD), F32)

    def one_head(h):
        own = head_of == h
        bias = bias_ref[h].reshape(N, N).astype(F32)
        head_rows = pl.ds(pl.multiple_of(h * DH, DH), DH)
        for r in range(2):
            rows = slice(r * N, (r + 1) * N)
            scores = s0_ref[r, h] + bias
            expo = jnp.exp(scores - jnp.max(scores, axis=1, keepdims=True))
            probs = expo * (1.0 / jnp.sum(expo, axis=1, keepdims=True))
            probs_low = probs.astype(BF16)
            att_ref[r] += dot(probs_low, jnp.where(own, v_ref[rows, :], none))
            d_probs = dp_ref[r, h]
            inner = jnp.sum(probs * d_probs, axis=1, keepdims=True)
            d_scores = probs * (d_probs - inner)
            low = d_scores.astype(BF16)
            dq_ref[r] += dot(low, jnp.where(own, k_ref[rows, :], none))
            dkt_ref[r, head_rows, :] = dot(qt_ref[r, head_rows, :], low)
            dvt_ref[r, head_rows, :] = dot(dat_ref[r, head_rows, :], probs_low)
            if r == 0:
                dbias_ref[h] = d_scores
            else:
                dbias_ref[h] += d_scores

    def rsc(t):
        return copy(sc_ref.at[t], rc_ref.at[t], rsc_s.at[t], rsc_r.at[t], partner)

    @pl.loop(0, HC)
    def _(t):
        one_head(far + t)
        sc_ref[t] = dbias_ref[far + t].reshape(NB, BR, N).astype(BF16)
        rsc(t).start()

    @pl.loop(0, HC)
    def _(t):
        handed(near, t).wait_recv()
        one_head(near + t)
        rsc(t).wait_recv()
        total = dbias_ref[near + t] + rc_ref[t].reshape(N, N).astype(F32)
        sa_ref[t] = total.reshape(NB, BR, N).astype(BF16)
        for b in plane:
            send(sa_ref.at[t, b], ra_ref.at[yx, t], rsa_s, rsa_r, yx_peer(b))

    later(ra_ref.at[pl.ds(0, NB - 1)], rsa_s)

    attended = att_ref[...].reshape(T, HD)
    gating = gate_ref[...]
    gated = (gating * attended).astype(BF16)
    update = dot(gated, ow_ref[...])
    next_pair = pair_ref[...].reshape(T, C).astype(F32) + update
    us_ref[...] = next_pair.astype(BF16).reshape(2, NB, BR, C)
    d_gate = dgated_ref[...] * attended * gating * (1.0 - gating)
    dproj_ref[:, 0:HD] = (dq_ref[...].reshape(T, HD) * scaling).astype(BF16)
    for r in range(2):
        rows = slice(r * N, (r + 1) * N)
        dproj_ref[rows, HD : 2 * HD] = jnp.transpose(dkt_ref[r]).astype(BF16)
        dproj_ref[rows, 2 * HD : 3 * HD] = jnp.transpose(dvt_ref[r]).astype(BF16)
    dproj_ref[:, 3 * HD :] = d_gate.astype(BF16)
    proj_part = dot(normed_ref[...], dproj_ref[...], TN)
    out_part = dot(gated, cot_ref[...].reshape(T, C), TN)
    wfull_ref[0] = proj_part[:, 0 : 3 * HD].reshape(16, 8, 3 * HD).astype(BF16)
    wfull_ref[1, :, :, 0:HD] = proj_part[:, 3 * HD :].reshape(16, 8, HD).astype(BF16)
    wfull_ref[1, :, :, HD : 2 * HD] = out_part.reshape(16, 8, HD).astype(BF16)
    wfull_ref[1, :, :, 2 * HD :] = jnp.zeros((16, 8, HD), BF16)
    wc = copy(wfull_ref.at[1 - c], wrc_ref, wc_s, wc_r, partner)
    wc.start()

    chain_sums = jnp.zeros((8, C), F32)
    lane = lax.broadcasted_iota(jnp.int32, (8, C), 1)
    row = lax.broadcasted_iota(jnp.int32, (8, C), 0)
    for h in range(H):
        value = jnp.sum(dbias_ref[h] * same_ref[...], axis=0, keepdims=True)
        value = jnp.sum(value, axis=1, keepdims=True)
        chain_sums = jnp.where((row == H) & (lane == h), value, chain_sums)

    wc.wait()
    own_half = wfull_ref[c].astype(F32) + wrc_ref[...].astype(F32)
    wsa_ref[...] = own_half.reshape(NB, 128 // NB, 3 * HD).astype(BF16)
    for b in plane:
        send(wsa_ref.at[b], wra_ref.at[yx], wa_s, wa_r, yx_peer(b))
    later(wra_ref.at[pl.ds(0, NB - 1)], wa_s)
    wra_ref[yx] = wsa_ref[yx]

    for b in plane:
        send(us_ref.at[:, b], ub_ref.at[yx], ua_s, ua_r, yx_peer(b))
    later(ub_ref.at[pl.ds(0, NB - 1)], ua_s)
    ub_ref[yx] = us_ref[:, yx]

    total = sa_ref[:, yx].astype(F32)
    arrived(ra_ref.at[pl.ds(0, NB - 1)], rsa_r)
    for b in plane:
        total = total + ra_ref[b].astype(F32)
    for g in range(G):
        for jl in range(2):
            sz_ref[g, jl * HC : (jl + 1) * HC, :] = total[:, 2 * g + jl, :]
    for g in column:
        send(sz_ref.at[g], rz_ref.at[zc], rsz_s, rsz_r, zc_peer(g))
    later(rz_ref.at[pl.ds(0, G - 1)], rsz_s)
    rz_ref[zc] = sz_ref[zc]

    arrived(wra_ref.at[pl.ds(0, NB - 1)], wa_r)
    wsum = wra_ref[0].astype(F32)
    for b in range(1, NB):
        wsum = wsum + wra_ref[b].astype(F32)
    wrz_ref[z] = wsum.astype(BF16)
    for zz in others(z, NZ):
        send(wrz_ref.at[z], wrz_ref.at[z], wz_s, wz_r, z_peer(zz))
    later(wrz_ref.at[pl.ds(0, NZ - 1)], wz_s)

    arrived(ub_ref.at[pl.ds(0, NB - 1)], ua_r)
    ux_ref[...] = ub_ref[...].reshape(NB * 2 * BR, C).astype(F32)
    for g in range(G):
        for jl in range(2):
            for r in range(2):
                start = r * BR + 2 * g + jl
                uz_ref[g, jl, r] = ux_ref[pl.ds(start, NB, stride=2 * BR), :].astype(BF16)
    for g in column:
        send(uz_ref.at[g], ur_ref.at[zc], uz_s, uz_r, zc_peer(g))
    later(ur_ref.at[pl.ds(0, G - 1)], uz_s)
    ur_ref[zc] = uz_ref[zc]

    d_normed = dot(dproj_ref[...], w_ref[...], NT)

    arrived(rz_ref.at[pl.ds(0, G - 1)], rsz_r)
    sums = []
    for core in range(NC):
        part = rz_ref[core]
        for zz in range(1, NZ):
            part = part + rz_ref[zz * NC + core]
        sums.append(part)
    d_bias = []
    for jl in range(2):
        d_bias.append(
            jnp.concatenate([s[jl * HC : (jl + 1) * HC] for s in sums], axis=0)
        )
    d_bias = jnp.concatenate(d_bias, axis=1)
    d_bias = jnp.concatenate([d_bias, jnp.zeros((8 - H, T), F32)], axis=0).astype(BF16)

    t0_ref[zc] = dot(d_bias, normed_ref[...]) + chain_sums
    for g in column:
        send(t0_ref.at[zc], t0_ref.at[zc], t0_s, t0_r, zc_peer(g))
    later(t0_ref.at[pl.ds(0, G - 1)], t0_s)

    d_normed = d_normed + dot(d_bias, bwt, TN)
    standard = std_ref[...]
    mean_grad = jnp.mean(d_normed, axis=-1, keepdims=True)
    mean_cross = jnp.mean(d_normed * standard, axis=-1, keepdims=True)
    pair_grad = (d_normed - mean_grad - standard * mean_cross) * inv_ref[...]
    pg_o[...] = pair_grad.astype(BF16)

    arrived(wrz_ref.at[pl.ds(0, NZ - 1)], wz_r)
    wsum = wrz_ref[0].astype(F32)
    for zz in range(1, NZ):
        wsum = wsum + wrz_ref[zz].astype(F32)
    wag_ref[c, yx] = wsum.astype(BF16)

    part = wag_ref.at[c, yx]
    for b in plane:
        send(part, part, wga_s, wga_r, yx_peer(b))
    most = wag_ref.at[c, pl.ds(0, NB - 1)]
    later(most, wga_s)

    arrived(t0_ref.at[pl.ds(0, G - 1)], t0_r)
    small = t0_ref[0]
    for g in range(1, G):
        small = small + t0_ref[g]
    t1_ref[yx] = small
    for b in plane:
        send(t1_ref.at[yx], t1_ref.at[yx], t1_s, t1_r, yx_peer(b))
    later(t1_ref.at[pl.ds(0, NB - 1)], t1_s)

    arrived(ur_ref.at[pl.ds(0, G - 1)], uz_r)
    for g in range(G):
        for jl in range(2):
            for r in range(2):
                start = jl * N + 2 * g + r
                npt_o[pl.ds(start, NB, stride=BR), :] = ur_ref[g, jl, r].astype(F32)

    arrived(most, wga_r)
    part = wag_ref.at[c]
    wgc = copy(part, part, wgc_s, wgc_r, partner)
    wgc.start()

    arrived(t1_ref.at[pl.ds(0, NB - 1)], t1_r)
    small = t1_ref[0]
    for b in range(1, NB):
        small = small + t1_ref[b]
    small_o[...] = small * (1.0 / N)
    wgc.wait_recv()
    wag_o[...] = wag_ref[...]

    wgc.wait_send()
    for d in drains:
        d.wait_send()
    for t in range(HC):
        rsc(t).wait_send()
        handed(far, t).wait_send()


def scratch(grid, N):
    NY, NX, NZ, NC = grid
    G, NB, HC = NZ * NC, NX * NY, H // NC
    BR, T, WR = 2 * G, 2 * N, 128 // NB
    V = pltpu.VMEM
    buffers = [
        V((1, H), F32),
        V((2, N, C), BF16),
        V((1, N), jnp.int32),
        V((1, N), jnp.int32),
        V((C, 4 * HD), BF16),
        V((H, C), BF16),
        V((HD, C), BF16),
        V((2, N, C), BF16),
        V((T, C), F32),
        V((T, C), F32),
        V((T, C), BF16),
        V((T, HD), BF16),
        V((T, HD), BF16),
        V((T, HD), BF16),
        V((T, HD), BF16),
        V((2, HD, N), BF16),
        V((2, HD, N), BF16),
        V((T, HD), F32),
        V((T, HD), F32),
        V((2, N, HD), F32),
        V((2, N, HD), F32),
        V((2, HD, N), F32),
        V((2, HD, N), F32),
        V((N, N), F32),
        V((H, N, N), F32),
        V((T, 4 * HD), BF16),
        V((2, H, N, N), F32),
        V((2, H, N, N), F32),
        V((G, 2 * H, N), BF16),
        V((H, NB, BR, N), BF16),
        V((HC, NB, BR, N), BF16),
        V((HC, NB, BR, N), BF16),
        V((HC, NB, BR, N), BF16),
        V((NB, HC, BR, N), BF16),
        V((G, 2 * HC, N), F32),
        V((G, 2 * HC, N), F32),
        V((NC, 16, 8, 3 * HD), BF16),
        V((16, 8, 3 * HD), BF16),
        V((NB, WR, 3 * HD), BF16),
        V((NB, WR, 3 * HD), BF16),
        V((NZ, WR, 3 * HD), BF16),
        V((NC, NB, WR, 3 * HD), BF16),
        V((2, NB, BR, C), BF16),
        V((NB, 2, BR, C), BF16),
        V((NB * 2 * BR, C), F32),
        V((G, 2, 2, NB, C), BF16),
        V((G, 2, 2, NB, C), BF16),
        V((G, 8, C), F32),
        V((NB, 8, C), F32),
    ]
    dma = pltpu.SemaphoreType.DMA
    pairs = [None] * 16
    pairs[3] = pairs[4] = (HC,)
    buffers.append(dma((8,)))
    for shape in pairs[1:]:
        buffers += [dma if shape is None else dma(shape)] * 2
    return buffers


def finish(npt_ref, pg_ref, wag_ref, small_ref, npt_o, pg_o, wg_o, bg_o, cg_o, og_o):
    N = npt_o.shape[1]
    npt_o[...] = npt_ref[...].reshape(2, N, C)
    pg_o[...] = pg_ref[...].reshape(2, N, C)
    scale = 1.0 / N
    first = wag_ref[0].astype(F32).reshape(C, 3 * HD) * scale
    second = wag_ref[1].astype(F32).reshape(C, 3 * HD) * scale
    wg_o[:, 0 : 3 * HD] = first
    wg_o[:, 3 * HD :] = second[:, 0:HD]
    og_o[...] = second[:, HD : 2 * HD]
    bg_o[...] = small_ref[0:H, :]
    cg_o[...] = small_ref[H : H + 1, 0:H]


def body(
    grid, pair, token_mask, chain_ids, proj_weight, bias_weight, chain_weight, out_weight, cotangent
):
    N = pair.shape[1]
    NY, NX, NZ, NC = grid
    vmem = pl.BlockSpec(memory_space=pltpu.VMEM)
    hbm = pl.BlockSpec(memory_space=pl.ANY)
    results = pl.pallas_call(
        functools.partial(kernel, grid, N),
        out_shape=(
            pltpu.VMEM((2 * N, C), F32),
            pltpu.VMEM((2 * N, C), BF16),
            pltpu.VMEM((NC, NX * NY, 128 // (NX * NY), 3 * HD), BF16),
            pltpu.VMEM((8, C), F32),
        ),
        in_specs=[hbm] * 8,
        out_specs=(vmem,) * 4,
        scratch_shapes=scratch(grid, N),
        compiler_params=pltpu.CompilerParams(collective_id=0, has_side_effects=True),
    )(
        chain_weight.reshape(1, H),
        pair,
        token_mask.reshape(1, N),
        chain_ids.reshape(1, N),
        proj_weight,
        jnp.transpose(bias_weight),
        out_weight,
        cotangent,
    )
    npt, pair_grad, weight_grad, bias_grad, chain_grad, out_grad = pl.pallas_call(
        finish,
        out_shape=(
            jax.ShapeDtypeStruct((2, N, C), F32),
            jax.ShapeDtypeStruct((2, N, C), BF16),
            jax.ShapeDtypeStruct((C, 4 * HD), F32),
            jax.ShapeDtypeStruct((H, C), F32),
            jax.ShapeDtypeStruct((1, H), F32),
            jax.ShapeDtypeStruct((HD, C), F32),
        ),
        in_specs=[vmem] * 4,
        out_specs=(vmem,) * 6,
    )(*[pltpu.with_memory_space_constraint(r, pltpu.VMEM) for r in results])
    return (
        npt,
        pair_grad,
        weight_grad,
        jnp.transpose(bias_grad),
        chain_grad.reshape(H),
        out_grad,
    )


def solution(mesh, grid=GRID):
    return jax.shard_map(
        functools.partial(body, grid),
        mesh=mesh,
        in_specs=(
            P(("dp", "dap"), None, None),
            P("dp"),
            P("dp"),
            P(),
            P(),
            P(),
            P(),
            P(("dp", "dap"), None, None),
        ),
        out_specs=(
            P(("dp", "dap"), None, None),
            P(("dp", "dap"), None, None),
            P("dp", None),
            P("dp", None),
            P("dp"),
            P("dp", None),
        ),
        check_vma=False,
    )
```

```python
import functools

import jax
import jax.numpy as jnp
from jax import lax
from jax.experimental import pallas as pl
from jax.experimental.pallas import tpu as pltpu
from jax.sharding import PartitionSpec as P

H = 4
DH = 32
HD = 128
C = 128
GRID = (4, 4, 4, 2)
EPSILON = 1e-05

F32 = jnp.float32
BF16 = jnp.bfloat16
NN = (((1,), (0,)), ((), ()))
NT = (((1,), (1,)), ((), ()))
TN = (((0,), (0,)), ((), ()))


def dot(a, b, dims=NN):
    return lax.dot_general(a, b, dims, preferred_element_type=F32)


def kernel(
    grid,
    tokens,
    cw_hbm,
    pair_hbm,
    mask_hbm,
    chain_hbm,
    w_hbm,
    bw_hbm,
    ow_hbm,
    cot_hbm,
    npt_o,
    pg_o,
    wag_o,
    small_o,
    cw_ref,
    pair_ref,
    mask_ref,
    chain_ref,
    w_ref,
    bw_ref,
    ow_ref,
    cot_ref,
    std_ref,
    inv_ref,
    normed_ref,
    q_ref,
    k_ref,
    v_ref,
    da_ref,
    qt_ref,
    dat_ref,
    gate_ref,
    dgated_ref,
    att_ref,
    dq_ref,
    dkt_ref,
    dvt_ref,
    same_ref,
    dbias_ref,
    dproj_ref,
    s0_ref,
    dp_ref,
    slot_ref,
    bias_ref,
    sc_ref,
    rc_ref,
    sa_ref,
    ra_ref,
    sz_ref,
    rz_ref,
    wfull_ref,
    wrc_ref,
    wsa_ref,
    wra_ref,
    wrz_ref,
    wag_ref,
    us_ref,
    ub_ref,
    ux_ref,
    uz_ref,
    ur_ref,
    t0_ref,
    t1_ref,
    rows_ref,
    in_s,
    slot_s,
    slot_r,
    ag_s,
    ag_r,
    agc_s,
    agc_r,
    rsc_s,
    rsc_r,
    rsa_s,
    rsa_r,
    rsz_s,
    rsz_r,
    wc_s,
    wc_r,
    wa_s,
    wa_r,
    wz_s,
    wz_r,
    wga_s,
    wga_r,
    wgc_s,
    wgc_r,
    ua_s,
    ua_r,
    uz_s,
    uz_r,
    t0_s,
    t0_r,
    t1_s,
    t1_r,
    nz_s,
    nz_r,
    nc_s,
    nc_r,
):
    NY, NX, NZ, NC = grid
    G = NZ * NC
    NB = NX * NY
    BR = 2 * G
    N = tokens
    T = 2 * N
    HC = H // NC

    idx = lax.axis_index("dap")
    zc = lax.rem(idx, G)
    c = lax.rem(idx, NC)
    z = lax.div(zc, NC)
    yx = lax.div(idx, G)
    x = lax.rem(yx, NX)
    y = lax.div(yx, NX)
    partner = idx + 1 - 2 * c
    far = HC * (1 - c)
    near = HC * c

    def zc_peer(g):
        return idx + g - zc

    def yx_peer(b):
        return idx + (b - yx) * G

    def z_peer(zz):
        return idx + (zz - z) * NC

    def others(me, n):
        return [lax.rem(me + d, n) for d in range(1, n)]

    steps = [(i, j) for i in range(NY) for j in range(NX) if i or j]
    steps.sort(key=lambda s: -min(s[0], NY - s[0]) - min(s[1], NX - s[1]))
    plane = [lax.rem(y + i, NY) * NX + lax.rem(x + j, NX) for i, j in steps]
    reach = list(range(1, G))
    reach.sort(key=lambda d: -min(d // NC, NZ - d // NC))
    column = [lax.rem(zc - c + d - d % NC, G) + lax.rem(c + d, NC) for d in reach]

    def copy(src, dst, ssem, rsem, dev):
        return pltpu.make_async_remote_copy(
            src_ref=src,
            dst_ref=dst,
            send_sem=ssem,
            recv_sem=rsem,
            device_id={"dap": dev},
            device_id_type=pl.DeviceIdType.MESH,
        )

    drains = []

    def send(src, dst, ssem, rsem, dev):
        copy(src, dst, ssem, rsem, dev).start()

    def arrived(ref, sem):
        copy(ref, ref, sem, sem, partner).wait_recv()

    def later(ref, sem):
        drains.append(copy(ref, ref, sem, sem, partner))

    barrier = pltpu.get_barrier_semaphore()
    peers = [zc_peer(g) for g in column] + [yx_peer(b) for b in plane]
    for p in peers:
        pl.semaphore_signal(
            barrier, inc=1, device_id={"dap": p}, device_id_type=pl.DeviceIdType.MESH
        )

    loads = []
    for number, (src, dst) in enumerate(
        (
            (pair_hbm, pair_ref),
            (bw_hbm, bw_ref),
            (w_hbm, w_ref),
            (cot_hbm, cot_ref),
            (ow_hbm, ow_ref),
            (chain_hbm, chain_ref),
            (mask_hbm, mask_ref),
            (cw_hbm, cw_ref),
        )
    ):
        d = pltpu.make_async_copy(src, dst, in_s.at[number])
        d.start()
        loads.append(d)
    loads[0].wait()

    values = pair_ref[...].reshape(T, C).astype(F32)
    centered = values - jnp.mean(values, axis=-1, keepdims=True)
    inverse = lax.rsqrt(jnp.mean(centered * centered, axis=-1, keepdims=True) + EPSILON)
    standard = centered * inverse
    std_ref[...] = standard
    inv_ref[...] = jnp.broadcast_to(inverse, (T, C))
    normed = standard.astype(BF16)
    normed_ref[...] = normed
    rows_ref[z, c] = normed
    loads[1].wait()
    bwt = jnp.concatenate([bw_ref[...].astype(F32), jnp.zeros((8 - H, C), F32)], axis=0)
    bwt = bwt.astype(BF16)
    local_bias = dot(bwt, normed, NT)
    slot_ref[zc] = jnp.concatenate(
        [local_bias[0:H, 0:N], local_bias[0:H, N:T]], axis=0
    ).astype(BF16)

    pl.semaphore_wait(barrier, len(peers))
    for g in column:
        send(slot_ref.at[zc], slot_ref.at[zc], slot_s, slot_r, zc_peer(g))
    later(slot_ref.at[pl.ds(0, G - 1)], slot_s)

    for d in loads[2:]:
        d.wait()
    projected = dot(normed, w_ref[...])
    scaling = DH ** (-0.5)
    q32 = projected[:, 0:HD] * scaling
    q_ref[...] = q32.astype(BF16)
    k_ref[...] = projected[:, HD : 2 * HD].astype(BF16)
    v_ref[...] = projected[:, 2 * HD : 3 * HD].astype(BF16)
    gating = jax.nn.sigmoid(projected[:, 3 * HD :])
    gate_ref[...] = gating
    d_gated = dot(cot_ref[...].reshape(T, C), ow_ref[...], NT)
    dgated_ref[...] = d_gated
    da32 = d_gated * gating
    da_ref[...] = da32.astype(BF16)
    for r in range(2):
        rows = slice(r * N, (r + 1) * N)
        qt_ref[r] = jnp.transpose(q32[rows]).astype(BF16)
        dat_ref[r] = jnp.transpose(da32[rows]).astype(BF16)

    chain = chain_ref[...].astype(F32)
    chain_cols = jnp.transpose(jnp.broadcast_to(chain, (HD, N)))
    chain_cols = jnp.concatenate([chain_cols] * (-(-N // HD)), axis=1)[:, 0:N]
    same_ref[...] = (chain_cols == jnp.broadcast_to(chain, (N, N))).astype(F32)
    masked = (mask_ref[...].astype(F32) - 1.0) * 1000000000.0
    head_of = lax.broadcasted_iota(jnp.int32, (N, HD), 1) // DH
    none = jnp.zeros((N, HD), BF16)

    @pl.loop(0, H)
    def _(h):
        own = head_of == h
        lane = lax.broadcasted_iota(jnp.int32, (1, H), 1) == h
        weight = jnp.sum(jnp.where(lane, cw_ref[...], 0.0), axis=1, keepdims=True)
        extra = weight * same_ref[...] + masked
        for r in range(2):
            rows = slice(r * N, (r + 1) * N)
            products = dot(jnp.where(own, q_ref[rows, :], none), k_ref[rows, :], NT)
            s0_ref[r, h] = products + extra
            dp_ref[r, h] = dot(jnp.where(own, da_ref[rows, :], none), v_ref[rows, :], NT)

    part = rows_ref.at[z, c]
    round_z = [lax.rem(z + d, NZ) for d in ((2, 1, 3) if NZ == 4 else range(1, NZ))]
    for number, zz in enumerate(round_z):
        send(part, part, nz_s, nz_r.at[number], z_peer(zz))
    later(rows_ref.at[pl.ds(0, NZ - 1), c], nz_s)

    def row_slot(zz):
        part = rows_ref.at[zz, c]
        send(part, part, nc_s, nc_r, partner)

    row_slot(z)

    arrived(slot_ref.at[pl.ds(0, G - 1)], slot_r)
    gathered = slot_ref[...].reshape(G * 2 * H, N)
    for t in range(HC):
        at = lax.broadcasted_iota(jnp.int32, (BR, G * 2 * H), 0) * H + (far + t)
        pick = (at == lax.broadcasted_iota(jnp.int32, (BR, G * 2 * H), 1)).astype(BF16)
        bias_ref[far + t, yx] = dot(pick, gathered).astype(BF16)

    part = bias_ref.at[pl.ds(far, HC), yx]
    for b in plane:
        send(part, part, ag_s, ag_r, yx_peer(b))
    most = bias_ref.at[pl.ds(far, HC), pl.ds(0, NB - 1)]
    later(most, ag_s)

    arrived(most, ag_r)

    def handed(first, t):
        part = bias_ref.at[first + t]
        return copy(part, part, agc_s.at[t], agc_r.at[t], partner)

    for t in range(HC):
        handed(far, t).start()

    att_ref[...] = jnp.zeros((2, N, HD), F32)
    dq_ref[...] = jnp.zeros((2, N, HD), F32)

    def one_head(h):
        own = head_of == h
        bias = bias_ref[h].reshape(N, N).astype(F32)
        head_rows = pl.ds(pl.multiple_of(h * DH, DH), DH)
        for r in range(2):
            rows = slice(r * N, (r + 1) * N)
            scores = s0_ref[r, h] + bias
            expo = jnp.exp(scores - jnp.max(scores, axis=1, keepdims=True))
            probs = expo * (1.0 / jnp.sum(expo, axis=1, keepdims=True))
            probs_low = probs.astype(BF16)
            att_ref[r] += dot(probs_low, jnp.where(own, v_ref[rows, :], none))
            d_probs = dp_ref[r, h]
            inner = jnp.sum(probs * d_probs, axis=1, keepdims=True)
            d_scores = probs * (d_probs - inner)
            low = d_scores.astype(BF16)
            dq_ref[r] += dot(low, jnp.where(own, k_ref[rows, :], none))
            dkt_ref[r, head_rows, :] = dot(qt_ref[r, head_rows, :], low)
            dvt_ref[r, head_rows, :] = dot(dat_ref[r, head_rows, :], probs_low)
            if r == 0:
                dbias_ref[h] = d_scores
            else:
                dbias_ref[h] += d_scores

    def rsc(t):
        return copy(sc_ref.at[t], rc_ref.at[t], rsc_s.at[t], rsc_r.at[t], partner)

    @pl.loop(0, HC)
    def _(t):
        one_head(far + t)
        sc_ref[t] = dbias_ref[far + t].reshape(NB, BR, N).astype(BF16)
        rsc(t).start()

    @pl.loop(0, HC)
    def _(t):
        handed(near, t).wait_recv()
        one_head(near + t)
        rsc(t).wait_recv()
        total = dbias_ref[near + t] + rc_ref[t].reshape(N, N).astype(F32)
        sa_ref[t] = total.reshape(NB, BR, N).astype(BF16)
        for b in plane:
            send(sa_ref.at[t, b], ra_ref.at[yx, t], rsa_s, rsa_r, yx_peer(b))

    later(ra_ref.at[pl.ds(0, NB - 1)], rsa_s)

    attended = att_ref[...].reshape(T, HD)
    gating = gate_ref[...]
    gated = (gating * attended).astype(BF16)
    update = dot(gated, ow_ref[...])
    next_pair = pair_ref[...].reshape(T, C).astype(F32) + update
    us_ref[...] = next_pair.astype(BF16).reshape(2, NB, BR, C)
    d_gate = dgated_ref[...] * attended * gating * (1.0 - gating)
    dproj_ref[:, 0:HD] = (dq_ref[...].reshape(T, HD) * scaling).astype(BF16)
    for r in range(2):
        rows = slice(r * N, (r + 1) * N)
        dproj_ref[rows, HD : 2 * HD] = jnp.transpose(dkt_ref[r]).astype(BF16)
        dproj_ref[rows, 2 * HD : 3 * HD] = jnp.transpose(dvt_ref[r]).astype(BF16)
    dproj_ref[:, 3 * HD :] = d_gate.astype(BF16)
    proj_part = dot(normed_ref[...], dproj_ref[...], TN)
    out_part = dot(gated, cot_ref[...].reshape(T, C), TN)
    wfull_ref[0] = proj_part[:, 0 : 3 * HD].reshape(16, 8, 3 * HD).astype(BF16)
    wfull_ref[1, :, :, 0:HD] = proj_part[:, 3 * HD :].reshape(16, 8, HD).astype(BF16)
    wfull_ref[1, :, :, HD : 2 * HD] = out_part.reshape(16, 8, HD).astype(BF16)
    wfull_ref[1, :, :, 2 * HD :] = jnp.zeros((16, 8, HD), BF16)
    wc = copy(wfull_ref.at[1 - c], wrc_ref, wc_s, wc_r, partner)
    wc.start()

    chain_sums = jnp.zeros((8, C), F32)
    lane = lax.broadcasted_iota(jnp.int32, (8, C), 1)
    row = lax.broadcasted_iota(jnp.int32, (8, C), 0)
    for h in range(H):
        value = jnp.sum(dbias_ref[h] * same_ref[...], axis=0, keepdims=True)
        value = jnp.sum(value, axis=1, keepdims=True)
        chain_sums = jnp.where((row == H) & (lane == h), value, chain_sums)

    wc.wait()
    own_half = wfull_ref[c].astype(F32) + wrc_ref[...].astype(F32)
    wsa_ref[...] = own_half.reshape(NB, 128 // NB, 3 * HD).astype(BF16)
    for b in plane:
        send(wsa_ref.at[b], wra_ref.at[yx], wa_s, wa_r, yx_peer(b))
    later(wra_ref.at[pl.ds(0, NB - 1)], wa_s)
    wra_ref[yx] = wsa_ref[yx]

    for b in plane:
        send(us_ref.at[:, b], ub_ref.at[yx], ua_s, ua_r, yx_peer(b))
    later(ub_ref.at[pl.ds(0, NB - 1)], ua_s)
    ub_ref[yx] = us_ref[:, yx]

    for number, d in enumerate((2, 3, 1) if NZ == 4 else range(NZ - 1, 0, -1)):
        zz = lax.rem(z + d, NZ)
        arrived(rows_ref.at[zz, c], nz_r.at[number])
        row_slot(zz)
    later(rows_ref.at[:, c], nc_s)

    total = sa_ref[:, yx].astype(F32)
    arrived(ra_ref.at[pl.ds(0, NB - 1)], rsa_r)
    for b in plane:
        total = total + ra_ref[b].astype(F32)
    for g in range(G):
        for jl in range(2):
            sz_ref[g, jl * HC : (jl + 1) * HC, :] = total[:, 2 * g + jl, :]

    wide = jnp.concatenate([total[:, i, :] for i in range(BR)], axis=1)
    row = lax.broadcasted_iota(jnp.int32, (8, BR * N), 0)
    parts = jnp.zeros((8, BR * N), F32)
    for t in range(HC):
        parts = jnp.where(row == near + t, wide[t : t + 1], parts)
    arrived(rows_ref.at[:, 1 - c], nc_r)
    small = dot(parts.astype(BF16), rows_ref[...].reshape(BR * N, C))
    t0_ref[zc] = small + chain_sums
    for g in column:
        send(t0_ref.at[zc], t0_ref.at[zc], t0_s, t0_r, zc_peer(g))
    later(t0_ref.at[pl.ds(0, G - 1)], t0_s)

    arrived(wra_ref.at[pl.ds(0, NB - 1)], wa_r)
    wsum = wra_ref[0].astype(F32)
    for b in range(1, NB):
        wsum = wsum + wra_ref[b].astype(F32)
    wrz_ref[z] = wsum.astype(BF16)
    for zz in others(z, NZ):
        send(wrz_ref.at[z], wrz_ref.at[z], wz_s, wz_r, z_peer(zz))
    later(wrz_ref.at[pl.ds(0, NZ - 1)], wz_s)

    for g in column:
        send(sz_ref.at[g], rz_ref.at[zc], rsz_s, rsz_r, zc_peer(g))
    later(rz_ref.at[pl.ds(0, G - 1)], rsz_s)
    rz_ref[zc] = sz_ref[zc]

    arrived(ub_ref.at[pl.ds(0, NB - 1)], ua_r)
    ux_ref[...] = ub_ref[...].reshape(NB * 2 * BR, C).astype(F32)
    for g in range(G):
        for jl in range(2):
            for r in range(2):
                start = r * BR + 2 * g + jl
                uz_ref[g, jl, r] = ux_ref[pl.ds(start, NB, stride=2 * BR), :].astype(BF16)
    for g in column:
        send(uz_ref.at[g], ur_ref.at[zc], uz_s, uz_r, zc_peer(g))
    later(ur_ref.at[pl.ds(0, G - 1)], uz_s)
    ur_ref[zc] = uz_ref[zc]

    d_normed = dot(dproj_ref[...], w_ref[...], NT)

    arrived(t0_ref.at[pl.ds(0, G - 1)], t0_r)
    small = t0_ref[0]
    for g in range(1, G):
        small = small + t0_ref[g]
    t1_ref[yx] = small
    for b in plane:
        send(t1_ref.at[yx], t1_ref.at[yx], t1_s, t1_r, yx_peer(b))
    later(t1_ref.at[pl.ds(0, NB - 1)], t1_s)

    arrived(wrz_ref.at[pl.ds(0, NZ - 1)], wz_r)
    wsum = wrz_ref[0].astype(F32)
    for zz in range(1, NZ):
        wsum = wsum + wrz_ref[zz].astype(F32)
    wag_ref[c, yx] = wsum.astype(BF16)

    part = wag_ref.at[c, yx]
    for b in plane:
        send(part, part, wga_s, wga_r, yx_peer(b))
    most = wag_ref.at[c, pl.ds(0, NB - 1)]
    later(most, wga_s)

    arrived(rz_ref.at[pl.ds(0, G - 1)], rsz_r)
    sums = []
    for core in range(NC):
        part = rz_ref[core]
        for zz in range(1, NZ):
            part = part + rz_ref[zz * NC + core]
        sums.append(part)
    d_bias = []
    for jl in range(2):
        d_bias.append(
            jnp.concatenate([s[jl * HC : (jl + 1) * HC] for s in sums], axis=0)
        )
    d_bias = jnp.concatenate(d_bias, axis=1)
    d_bias = jnp.concatenate([d_bias, jnp.zeros((8 - H, T), F32)], axis=0).astype(BF16)

    d_normed = d_normed + dot(d_bias, bwt, TN)
    standard = std_ref[...]
    mean_grad = jnp.mean(d_normed, axis=-1, keepdims=True)
    mean_cross = jnp.mean(d_normed * standard, axis=-1, keepdims=True)
    pair_grad = (d_normed - mean_grad - standard * mean_cross) * inv_ref[...]
    pg_o[...] = pair_grad.astype(BF16)

    arrived(most, wga_r)
    part = wag_ref.at[c]
    wgc = copy(part, part, wgc_s, wgc_r, partner)
    wgc.start()

    arrived(ur_ref.at[pl.ds(0, G - 1)], uz_r)
    for g in range(G):
        for jl in range(2):
            for r in range(2):
                start = jl * N + 2 * g + r
                npt_o[pl.ds(start, NB, stride=BR), :] = ur_ref[g, jl, r].astype(F32)

    arrived(t1_ref.at[pl.ds(0, NB - 1)], t1_r)
    small = t1_ref[0]
    for b in range(1, NB):
        small = small + t1_ref[b]
    small_o[...] = small * (1.0 / N)
    wgc.wait_recv()
    wag_o[...] = wag_ref[...]

    wgc.wait_send()
    for d in drains:
        d.wait_send()
    for t in range(HC):
        rsc(t).wait_send()
        handed(far, t).wait_send()


def scratch(grid, N):
    NY, NX, NZ, NC = grid
    G, NB, HC = NZ * NC, NX * NY, H // NC
    BR, T, WR = 2 * G, 2 * N, 128 // NB
    V = pltpu.VMEM
    buffers = [
        V((1, H), F32),
        V((2, N, C), BF16),
        V((1, N), jnp.int32),
        V((1, N), jnp.int32),
        V((C, 4 * HD), BF16),
        V((H, C), BF16),
        V((HD, C), BF16),
        V((2, N, C), BF16),
        V((T, C), F32),
        V((T, C), F32),
        V((T, C), BF16),
        V((T, HD), BF16),
        V((T, HD), BF16),
        V((T, HD), BF16),
        V((T, HD), BF16),
        V((2, HD, N), BF16),
        V((2, HD, N), BF16),
        V((T, HD), F32),
        V((T, HD), F32),
        V((2, N, HD), F32),
        V((2, N, HD), F32),
        V((2, HD, N), F32),
        V((2, HD, N), F32),
        V((N, N), F32),
        V((H, N, N), F32),
        V((T, 4 * HD), BF16),
        V((2, H, N, N), F32),
        V((2, H, N, N), F32),
        V((G, 2 * H, N), BF16),
        V((H, NB, BR, N), BF16),
        V((HC, NB, BR, N), BF16),
        V((HC, NB, BR, N), BF16),
        V((HC, NB, BR, N), BF16),
        V((NB, HC, BR, N), BF16),
        V((G, 2 * HC, N), F32),
        V((G, 2 * HC, N), F32),
        V((NC, 16, 8, 3 * HD), BF16),
        V((16, 8, 3 * HD), BF16),
        V((NB, WR, 3 * HD), BF16),
        V((NB, WR, 3 * HD), BF16),
        V((NZ, WR, 3 * HD), BF16),
        V((NC, NB, WR, 3 * HD), BF16),
        V((2, NB, BR, C), BF16),
        V((NB, 2, BR, C), BF16),
        V((NB * 2 * BR, C), F32),
        V((G, 2, 2, NB, C), BF16),
        V((G, 2, 2, NB, C), BF16),
        V((G, 8, C), F32),
        V((NB, 8, C), F32),
        V((NZ, NC, T, C), BF16),
    ]
    dma = pltpu.SemaphoreType.DMA
    pairs = [None] * 16
    pairs[3] = pairs[4] = (HC,)
    buffers.append(dma((8,)))
    for shape in pairs[1:16]:
        buffers += [dma if shape is None else dma(shape)] * 2
    buffers += [dma, dma((NZ,)), dma, dma]
    return buffers


def finish(npt_ref, pg_ref, wag_ref, small_ref, npt_o, pg_o, wg_o, bg_o, cg_o, og_o):
    N = npt_o.shape[1]
    npt_o[...] = npt_ref[...].reshape(2, N, C)
    pg_o[...] = pg_ref[...].reshape(2, N, C)
    scale = 1.0 / N
    first = wag_ref[0].astype(F32).reshape(C, 3 * HD) * scale
    second = wag_ref[1].astype(F32).reshape(C, 3 * HD) * scale
    wg_o[:, 0 : 3 * HD] = first
    wg_o[:, 3 * HD :] = second[:, 0:HD]
    og_o[...] = second[:, HD : 2 * HD]
    bg_o[...] = small_ref[0:H, :]
    cg_o[...] = small_ref[H : H + 1, 0:H]


def body(
    grid, pair, token_mask, chain_ids, proj_weight, bias_weight, chain_weight, out_weight, cotangent
):
    N = pair.shape[1]
    NY, NX, NZ, NC = grid
    vmem = pl.BlockSpec(memory_space=pltpu.VMEM)
    hbm = pl.BlockSpec(memory_space=pl.ANY)
    results = pl.pallas_call(
        functools.partial(kernel, grid, N),
        out_shape=(
            pltpu.VMEM((2 * N, C), F32),
            pltpu.VMEM((2 * N, C), BF16),
            pltpu.VMEM((NC, NX * NY, 128 // (NX * NY), 3 * HD), BF16),
            pltpu.VMEM((8, C), F32),
        ),
        in_specs=[hbm] * 8,
        out_specs=(vmem,) * 4,
        scratch_shapes=scratch(grid, N),
        compiler_params=pltpu.CompilerParams(collective_id=0, has_side_effects=True),
    )(
        chain_weight.reshape(1, H),
        pair,
        token_mask.reshape(1, N),
        chain_ids.reshape(1, N),
        proj_weight,
        jnp.transpose(bias_weight),
        out_weight,
        cotangent,
    )
    npt, pair_grad, weight_grad, bias_grad, chain_grad, out_grad = pl.pallas_call(
        finish,
        out_shape=(
            jax.ShapeDtypeStruct((2, N, C), F32),
            jax.ShapeDtypeStruct((2, N, C), BF16),
            jax.ShapeDtypeStruct((C, 4 * HD), F32),
            jax.ShapeDtypeStruct((H, C), F32),
            jax.ShapeDtypeStruct((1, H), F32),
            jax.ShapeDtypeStruct((HD, C), F32),
        ),
        in_specs=[vmem] * 4,
        out_specs=(vmem,) * 6,
    )(*[pltpu.with_memory_space_constraint(r, pltpu.VMEM) for r in results])
    return (
        npt,
        pair_grad,
        weight_grad,
        jnp.transpose(bias_grad),
        chain_grad.reshape(H),
        out_grad,
    )


def solution(mesh, grid=GRID):
    return jax.shard_map(
        functools.partial(body, grid),
        mesh=mesh,
        in_specs=(
            P(("dp", "dap"), None, None),
            P("dp"),
            P("dp"),
            P(),
            P(),
            P(),
            P(),
            P(("dp", "dap"), None, None),
        ),
        out_specs=(
            P(("dp", "dap"), None, None),
            P(("dp", "dap"), None, None),
            P("dp", None),
            P("dp", None),
            P("dp"),
            P("dp", None),
        ),
        check_vma=False,
    )
```

```python
import functools

import jax
import jax.numpy as jnp
from jax import lax
from jax.experimental import pallas as pl
from jax.experimental.pallas import tpu as pltpu
from jax.sharding import PartitionSpec as P

H = 4
DH = 32
HD = 128
C = 128
GRID = (4, 4, 4, 2)
EPSILON = 1e-05

F32 = jnp.float32
BF16 = jnp.bfloat16
NN = (((1,), (0,)), ((), ()))
NT = (((1,), (1,)), ((), ()))
TN = (((0,), (0,)), ((), ()))


def dot(a, b, dims=NN):
    return lax.dot_general(a, b, dims, preferred_element_type=F32)


def kernel(
    grid,
    tokens,
    cw_hbm,
    pair_hbm,
    mask_hbm,
    chain_hbm,
    w_hbm,
    bw_hbm,
    ow_hbm,
    cot_hbm,
    npt_o,
    pg_o,
    wag_o,
    small_o,
    cw_ref,
    pair_ref,
    mask_ref,
    chain_ref,
    w_ref,
    bw_ref,
    ow_ref,
    cot_ref,
    std_ref,
    inv_ref,
    q_ref,
    k_ref,
    v_ref,
    da_ref,
    qt_ref,
    dat_ref,
    gate_ref,
    dgated_ref,
    att_ref,
    dq_ref,
    dkv_ref,
    same_ref,
    dbias_ref,
    dproj_ref,
    s0_ref,
    dp_ref,
    slot_ref,
    bias_ref,
    sa_ref,
    ra_ref,
    sz_ref,
    rz_ref,
    wsa_ref,
    wra_ref,
    wrz_ref,
    wag_ref,
    us_ref,
    ub_ref,
    ux_ref,
    uz_ref,
    ur_ref,
    t0_ref,
    t1_ref,
    rows_ref,
    u32_ref,
    u16_ref,
    up_ref,
    d16_ref,
    dn_ref,
    wc_ref,
    outp_ref,
    in_s,
    slot_s,
    slot_r,
    ag_s,
    ag_r,
    rsa_s,
    rsa_r,
    rsz_s,
    rsz_r,
    wa_s,
    wa_r,
    wz_s,
    wz_r,
    wga_s,
    wga_r,
    wgc_s,
    wgc_r,
    ua_s,
    ua_r,
    uz_s,
    uz_r,
    t0_s,
    t0_r,
    t1_s,
    t1_r,
    pn_s,
    pn_r,
    pc_s,
    pc_r,
    up_s,
    up_r,
    dn_s,
    dn_r,
    nz_s,
    nz_r,
    nc_s,
    nc_r,
):
    NY, NX, NZ, NC = grid
    G = NZ * NC
    NB = NX * NY
    BR = 2 * G
    N = tokens
    T = 2 * N
    HC = H // NC

    idx = lax.axis_index("dap")
    zc = lax.rem(idx, G)
    c = lax.rem(idx, NC)
    z = lax.div(zc, NC)
    yx = lax.div(idx, G)
    x = lax.rem(yx, NX)
    y = lax.div(yx, NX)
    partner = idx + 1 - 2 * c
    near = HC * c
    HW = HC * DH

    def zc_peer(g):
        return idx + g - zc

    def yx_peer(b):
        return idx + (b - yx) * G

    def z_peer(zz):
        return idx + (zz - z) * NC

    def others(me, n):
        return [lax.rem(me + d, n) for d in range(1, n)]

    steps = [(i, j) for i in range(NY) for j in range(NX) if i or j]
    steps.sort(key=lambda s: -min(s[0], NY - s[0]) - min(s[1], NX - s[1]))
    plane = [lax.rem(y + i, NY) * NX + lax.rem(x + j, NX) for i, j in steps]
    reach = list(range(1, G))
    reach.sort(key=lambda d: -min(d // NC, NZ - d // NC))
    column = [lax.rem(zc - c + d - d % NC, G) + lax.rem(c + d, NC) for d in reach]

    def copy(src, dst, ssem, rsem, dev):
        return pltpu.make_async_remote_copy(
            src_ref=src,
            dst_ref=dst,
            send_sem=ssem,
            recv_sem=rsem,
            device_id={"dap": dev},
            device_id_type=pl.DeviceIdType.MESH,
        )

    drains = []

    def send(src, dst, ssem, rsem, dev):
        copy(src, dst, ssem, rsem, dev).start()

    def arrived(ref, sem):
        copy(ref, ref, sem, sem, partner).wait_recv()

    def later(ref, sem):
        drains.append(copy(ref, ref, sem, sem, partner))

    barrier = pltpu.get_barrier_semaphore()
    peers = [zc_peer(g) for g in column] + [yx_peer(b) for b in plane]
    for p in peers:
        pl.semaphore_signal(
            barrier, inc=1, device_id={"dap": p}, device_id_type=pl.DeviceIdType.MESH
        )

    loads = []
    for number, (src, dst) in enumerate(
        (
            (pair_hbm, pair_ref),
            (bw_hbm, bw_ref),
            (w_hbm, w_ref),
            (cot_hbm, cot_ref.at[c]),
            (ow_hbm, ow_ref),
            (chain_hbm, chain_ref),
            (mask_hbm, mask_ref),
            (cw_hbm, cw_ref),
        )
    ):
        d = pltpu.make_async_copy(src, dst, in_s.at[number])
        d.start()
        loads.append(d)
    loads[0].wait()

    values = pair_ref[...].reshape(T, C).astype(F32)
    centered = values - jnp.mean(values, axis=-1, keepdims=True)
    inverse = lax.rsqrt(jnp.mean(centered * centered, axis=-1, keepdims=True) + EPSILON)
    standard = centered * inverse
    std_ref[...] = standard
    inv_ref[...] = jnp.broadcast_to(inverse, (T, C))
    normed = standard.astype(BF16)
    rows_ref[z, c] = normed
    loads[1].wait()
    bwt = jnp.concatenate([bw_ref[...].astype(F32), jnp.zeros((8 - H, C), F32)], axis=0)
    bwt = bwt.astype(BF16)
    local_bias = dot(bwt, normed, NT)
    slot_ref[zc] = jnp.concatenate(
        [local_bias[0:H, 0:N], local_bias[0:H, N:T]], axis=0
    ).astype(BF16)

    pl.semaphore_wait(barrier, len(peers))
    for g in column:
        send(slot_ref.at[zc], slot_ref.at[zc], slot_s, slot_r, zc_peer(g))
    later(slot_ref.at[pl.ds(0, G - 1)], slot_s)
    part = rows_ref.at[z, c]
    send(part, part, pn_s, pn_r, partner)
    later(part, pn_s)
    for d in loads[2:]:
        d.wait()
    send(cot_ref.at[c], cot_ref.at[c], pc_s, pc_r, partner)
    later(cot_ref.at[c], pc_s)

    scaling = DH ** (-0.5)

    def project(core):
        projected = dot(rows_ref[z, core], w_ref[...])
        q32 = projected[:, 0:HD] * scaling
        q_ref[core] = q32.astype(BF16)
        k_ref[core] = projected[:, HD : 2 * HD].astype(BF16)
        v_ref[core] = projected[:, 2 * HD : 3 * HD].astype(BF16)
        gating = jax.nn.sigmoid(projected[:, 3 * HD :])
        gate_ref[core] = gating
        d_gated = dot(cot_ref[core].reshape(T, C), ow_ref[...], NT)
        dgated_ref[core] = d_gated
        da32 = d_gated * gating
        da_ref[core] = da32.astype(BF16)
        for r in range(2):
            rows = slice(r * N, (r + 1) * N)
            qt_ref[core, r] = jnp.transpose(q32[rows]).astype(BF16)
            dat_ref[core, r] = jnp.transpose(da32[rows]).astype(BF16)

    project(c)
    arrived(rows_ref.at[z, 1 - c], pn_r)
    arrived(cot_ref.at[1 - c], pc_r)
    project(1 - c)

    part = rows_ref.at[z, c]
    round_z = [lax.rem(z + d, NZ) for d in ((2, 1, 3) if NZ == 4 else range(1, NZ))]
    for number, zz in enumerate(round_z):
        send(part, part, nz_s, nz_r.at[number], z_peer(zz))
    later(rows_ref.at[pl.ds(0, NZ - 1), c], nz_s)

    def row_slot(zz):
        part = rows_ref.at[zz, c]
        send(part, part, nc_s, nc_r, partner)

    chain = chain_ref[...].astype(F32)
    chain_cols = jnp.transpose(jnp.broadcast_to(chain, (HD, N)))
    chain_cols = jnp.concatenate([chain_cols] * (-(-N // HD)), axis=1)[:, 0:N]
    same_ref[...] = (chain_cols == jnp.broadcast_to(chain, (N, N))).astype(F32)
    masked = (mask_ref[...].astype(F32) - 1.0) * 1000000000.0
    head_of = lax.broadcasted_iota(jnp.int32, (N, HD), 1) // DH
    none = jnp.zeros((N, HD), BF16)

    @pl.loop(0, HC)
    def _(t):
        h = near + t
        own = head_of == h
        lane = lax.broadcasted_iota(jnp.int32, (1, H), 1) == h
        weight = jnp.sum(jnp.where(lane, cw_ref[...], 0.0), axis=1, keepdims=True)
        extra = weight * same_ref[...] + masked
        for core in range(NC):
            for r in range(2):
                rows = slice(r * N, (r + 1) * N)
                query = jnp.where(own, q_ref[core, rows, :], none)
                s0_ref[t, core, r] = dot(query, k_ref[core, rows, :], NT) + extra
                grad = jnp.where(own, da_ref[core, rows, :], none)
                dp_ref[t, core, r] = dot(grad, v_ref[core, rows, :], NT)

    arrived(slot_ref.at[pl.ds(0, G - 1)], slot_r)
    gathered = slot_ref[...].reshape(G * 2 * H, N)
    for t in range(HC):
        at = lax.broadcasted_iota(jnp.int32, (BR, G * 2 * H), 0) * H + (near + t)
        pick = (at == lax.broadcasted_iota(jnp.int32, (BR, G * 2 * H), 1)).astype(BF16)
        bias_ref[t, yx] = dot(pick, gathered).astype(BF16)

    for b in plane:
        send(bias_ref.at[:, yx], bias_ref.at[:, yx], ag_s, ag_r, yx_peer(b))
    most = bias_ref.at[:, pl.ds(0, NB - 1)]
    later(most, ag_s)

    arrived(most, ag_r)

    att_ref[...] = jnp.zeros((NC, 2, N, HD), F32)
    dq_ref[...] = jnp.zeros((NC, 2, N, HD), F32)

    @pl.loop(0, HC)
    def _(t):
        h = near + t
        own = head_of == h
        bias = bias_ref[t].reshape(N, N).astype(F32)
        head_rows = pl.ds(pl.multiple_of(h * DH, DH), DH)
        key_rows = pl.ds(pl.multiple_of(t * DH, DH), DH)
        value_rows = pl.ds(pl.multiple_of(HW + t * DH, DH), DH)
        for core in range(NC):
            for r in range(2):
                rows = slice(r * N, (r + 1) * N)
                scores = s0_ref[t, core, r] + bias
                expo = jnp.exp(scores - jnp.max(scores, axis=1, keepdims=True))
                probs = expo * (1.0 / jnp.sum(expo, axis=1, keepdims=True))
                probs_low = probs.astype(BF16)
                values = jnp.where(own, v_ref[core, rows, :], none)
                att_ref[core, r] += dot(probs_low, values)
                d_probs = dp_ref[t, core, r]
                inner = jnp.sum(probs * d_probs, axis=1, keepdims=True)
                d_scores = probs * (d_probs - inner)
                low = d_scores.astype(BF16)
                dq_ref[core, r] += dot(low, jnp.where(own, k_ref[core, rows, :], none))
                dkv_ref[core, r, key_rows, :] = dot(qt_ref[core, r, head_rows, :], low)
                dkv_ref[core, r, value_rows, :] = dot(
                    dat_ref[core, r, head_rows, :], probs_low
                )
                if core == 0 and r == 0:
                    dbias_ref[t] = d_scores
                else:
                    dbias_ref[t] += d_scores
        sa_ref[t] = dbias_ref[t].reshape(NB, BR, N).astype(BF16)
        for b in plane:
            send(sa_ref.at[t, b], ra_ref.at[yx, t], rsa_s, rsa_r, yx_peer(b))

    later(ra_ref.at[pl.ds(0, NB - 1)], rsa_s)

    rows_all = NC * T
    attended = att_ref[...].reshape(rows_all, HD)
    gating = gate_ref[...].reshape(rows_all, HD)
    gated = (gating * attended).astype(BF16)
    d_gate = dgated_ref[...].reshape(rows_all, HD) * attended * gating * (1.0 - gating)
    d_query = dq_ref[...].reshape(rows_all, HD) * scaling
    mine = lax.broadcasted_iota(jnp.int32, (rows_all, HD), 1) // HW == c
    both = jnp.where(mine, d_query, pltpu.roll(d_gate, HW, 1))
    dproj_ref[:, 0:HD] = both.astype(BF16)
    for core in range(NC):
        for r in range(2):
            rows = slice((core * 2 + r) * N, (core * 2 + r + 1) * N)
            dproj_ref[rows, HD:] = jnp.transpose(dkv_ref[core, r]).astype(BF16)
    normed_all = rows_ref[z].reshape(rows_all, C)
    proj_part = dot(normed_all, dproj_ref[...], TN)
    outp_ref[...] = dot(gated, cot_ref[...].reshape(rows_all, C), TN)
    out_part = outp_ref[pl.ds(pl.multiple_of(c * HW, HW), HW), :]
    out_part = jnp.concatenate([out_part, jnp.zeros((C - HW, C), F32)], axis=0)
    wsa = jnp.concatenate([proj_part, out_part], axis=1)
    wsa_ref[...] = wsa.reshape(NB, C // NB, 3 * HD).astype(BF16)
    for b in plane:
        send(wsa_ref.at[b], wra_ref.at[yx], wa_s, wa_r, yx_peer(b))
    later(wra_ref.at[pl.ds(0, NB - 1)], wa_s)
    wra_ref[yx] = wsa_ref[yx]

    update = dot(gated, ow_ref[...])
    u32_ref[...] = update.reshape(NC, T, C)
    u16_ref[...] = u32_ref[1 - c].astype(BF16)
    send(u16_ref, up_ref, up_s, up_r, partner)
    later(u16_ref, up_s)

    chain_sums = jnp.zeros((8, C), F32)
    lane = lax.broadcasted_iota(jnp.int32, (8, C), 1)
    row = lax.broadcasted_iota(jnp.int32, (8, C), 0)
    for t in range(HC):
        value = jnp.sum(dbias_ref[t] * same_ref[...], axis=0, keepdims=True)
        value = jnp.sum(value, axis=1, keepdims=True)
        chain_sums = jnp.where((row == H) & (lane == near + t), value, chain_sums)

    arrived(up_ref, up_r)
    update = u32_ref[c] + up_ref[...].astype(F32)
    next_pair = pair_ref[...].reshape(T, C).astype(F32) + update
    us_ref[...] = next_pair.astype(BF16).reshape(2, NB, BR, C)
    for b in plane:
        send(us_ref.at[:, b], ub_ref.at[yx], ua_s, ua_r, yx_peer(b))
    later(ub_ref.at[pl.ds(0, NB - 1)], ua_s)
    ub_ref[yx] = us_ref[:, yx]

    for number, d in enumerate((2, 3, 1) if NZ == 4 else range(NZ - 1, 0, -1)):
        zz = lax.rem(z + d, NZ)
        arrived(rows_ref.at[zz, c], nz_r.at[number])
        row_slot(zz)
    later(rows_ref.at[pl.ds(0, NZ - 1), c], nc_s)

    total = sa_ref[:, yx].astype(F32)
    arrived(ra_ref.at[pl.ds(0, NB - 1)], rsa_r)
    for b in plane:
        total = total + ra_ref[b].astype(F32)
    for g in range(G):
        for jl in range(2):
            sz_ref[g, jl * HC : (jl + 1) * HC, :] = total[:, 2 * g + jl, :]

    wide = jnp.concatenate([total[:, i, :] for i in range(BR)], axis=1)
    row = lax.broadcasted_iota(jnp.int32, (8, BR * N), 0)
    parts = jnp.zeros((8, BR * N), F32)
    for t in range(HC):
        parts = jnp.where(row == near + t, wide[t : t + 1], parts)
    arrived(rows_ref.at[pl.ds(0, NZ - 1), 1 - c], nc_r)
    small = dot(parts.astype(BF16), rows_ref[...].reshape(BR * N, C))
    t0_ref[zc] = small + chain_sums
    for g in column:
        send(t0_ref.at[zc], t0_ref.at[zc], t0_s, t0_r, zc_peer(g))
    later(t0_ref.at[pl.ds(0, G - 1)], t0_s)

    arrived(wra_ref.at[pl.ds(0, NB - 1)], wa_r)
    wsum = wra_ref[0].astype(F32)
    for b in range(1, NB):
        wsum = wsum + wra_ref[b].astype(F32)
    wrz_ref[z] = wsum.astype(BF16)
    for zz in others(z, NZ):
        send(wrz_ref.at[z], wrz_ref.at[z], wz_s, wz_r, z_peer(zz))
    later(wrz_ref.at[pl.ds(0, NZ - 1)], wz_s)

    for g in column:
        send(sz_ref.at[g], rz_ref.at[zc], rsz_s, rsz_r, zc_peer(g))
    later(rz_ref.at[pl.ds(0, G - 1)], rsz_s)
    rz_ref[zc] = sz_ref[zc]

    arrived(ub_ref.at[pl.ds(0, NB - 1)], ua_r)
    ux_ref[...] = ub_ref[...].reshape(NB * 2 * BR, C).astype(F32)
    for g in range(G):
        for jl in range(2):
            for r in range(2):
                start = r * BR + 2 * g + jl
                uz_ref[g, jl, r] = ux_ref[pl.ds(start, NB, stride=2 * BR), :].astype(BF16)
    for g in column:
        send(uz_ref.at[g], ur_ref.at[zc], uz_s, uz_r, zc_peer(g))
    later(ur_ref.at[pl.ds(0, G - 1)], uz_s)
    ur_ref[zc] = uz_ref[zc]

    first = lax.broadcasted_iota(jnp.int32, (C, HD), 1) < HW
    own_lanes = lax.broadcasted_iota(jnp.int32, (C, HD), 1) // HW == c
    weights = [w_ref[:, i * HD : (i + 1) * HD].astype(F32) for i in range(4)]
    swapped = [pltpu.roll(v, HW, 1) for v in weights]
    pick_k = jnp.where(c == 0, weights[1], swapped[1])
    pick_v = jnp.where(c == 0, swapped[2], weights[2])
    wc_ref[:, 0:HD] = jnp.where(own_lanes, weights[0], swapped[3]).astype(BF16)
    wc_ref[:, HD:] = jnp.where(first, pick_k, pick_v).astype(BF16)
    u32_ref[...] = dot(dproj_ref[...], wc_ref[...], NT).reshape(NC, T, C)
    d16_ref[...] = u32_ref[1 - c].astype(BF16)
    send(d16_ref, dn_ref, dn_s, dn_r, partner)
    later(d16_ref, dn_s)

    arrived(t0_ref.at[pl.ds(0, G - 1)], t0_r)
    small = t0_ref[0]
    for g in range(1, G):
        small = small + t0_ref[g]
    t1_ref[yx] = small
    for b in plane:
        send(t1_ref.at[yx], t1_ref.at[yx], t1_s, t1_r, yx_peer(b))
    later(t1_ref.at[pl.ds(0, NB - 1)], t1_s)

    arrived(wrz_ref.at[pl.ds(0, NZ - 1)], wz_r)
    wsum = wrz_ref[0].astype(F32)
    for zz in range(1, NZ):
        wsum = wsum + wrz_ref[zz].astype(F32)
    wag_ref[c, yx] = wsum.astype(BF16)

    part = wag_ref.at[c, yx]
    for b in plane:
        send(part, part, wga_s, wga_r, yx_peer(b))
    most = wag_ref.at[c, pl.ds(0, NB - 1)]
    later(most, wga_s)

    arrived(rz_ref.at[pl.ds(0, G - 1)], rsz_r)
    sums = []
    for core in range(NC):
        part = rz_ref[core]
        for zz in range(1, NZ):
            part = part + rz_ref[zz * NC + core]
        sums.append(part)
    d_bias = []
    for jl in range(2):
        d_bias.append(
            jnp.concatenate([s[jl * HC : (jl + 1) * HC] for s in sums], axis=0)
        )
    d_bias = jnp.concatenate(d_bias, axis=1)
    d_bias = jnp.concatenate([d_bias, jnp.zeros((8 - H, T), F32)], axis=0).astype(BF16)

    arrived(dn_ref, dn_r)
    d_normed = u32_ref[c] + dn_ref[...].astype(F32) + dot(d_bias, bwt, TN)
    standard = std_ref[...]
    mean_grad = jnp.mean(d_normed, axis=-1, keepdims=True)
    mean_cross = jnp.mean(d_normed * standard, axis=-1, keepdims=True)
    pair_grad = (d_normed - mean_grad - standard * mean_cross) * inv_ref[...]
    pg_o[...] = pair_grad.astype(BF16)

    arrived(most, wga_r)
    part = wag_ref.at[c]
    wgc = copy(part, part, wgc_s, wgc_r, partner)
    wgc.start()

    arrived(ur_ref.at[pl.ds(0, G - 1)], uz_r)
    for g in range(G):
        for jl in range(2):
            for r in range(2):
                start = jl * N + 2 * g + r
                npt_o[pl.ds(start, NB, stride=BR), :] = ur_ref[g, jl, r].astype(F32)

    arrived(t1_ref.at[pl.ds(0, NB - 1)], t1_r)
    small = t1_ref[0]
    for b in range(1, NB):
        small = small + t1_ref[b]
    small_o[...] = small * (1.0 / N)
    wgc.wait_recv()
    wag_o[...] = wag_ref[...]

    wgc.wait_send()
    for d in drains:
        d.wait_send()


def scratch(grid, N):
    NY, NX, NZ, NC = grid
    G, NB, HC = NZ * NC, NX * NY, H // NC
    BR, T, WR = 2 * G, 2 * N, 128 // NB
    V = pltpu.VMEM
    buffers = [
        V((1, H), F32),
        V((2, N, C), BF16),
        V((1, N), jnp.int32),
        V((1, N), jnp.int32),
        V((C, 4 * HD), BF16),
        V((H, C), BF16),
        V((HD, C), BF16),
        V((NC, 2, N, C), BF16),
        V((T, C), F32),
        V((T, C), F32),
        V((NC, T, HD), BF16),
        V((NC, T, HD), BF16),
        V((NC, T, HD), BF16),
        V((NC, T, HD), BF16),
        V((NC, 2, HD, N), BF16),
        V((NC, 2, HD, N), BF16),
        V((NC, T, HD), F32),
        V((NC, T, HD), F32),
        V((NC, 2, N, HD), F32),
        V((NC, 2, N, HD), F32),
        V((NC, 2, HD, N), F32),
        V((N, N), F32),
        V((HC, N, N), F32),
        V((NC * T, 2 * HD), BF16),
        V((HC, NC, 2, N, N), F32),
        V((HC, NC, 2, N, N), F32),
        V((G, 2 * H, N), BF16),
        V((HC, NB, BR, N), BF16),
        V((HC, NB, BR, N), BF16),
        V((NB, HC, BR, N), BF16),
        V((G, 2 * HC, N), F32),
        V((G, 2 * HC, N), F32),
        V((NB, WR, 3 * HD), BF16),
        V((NB, WR, 3 * HD), BF16),
        V((NZ, WR, 3 * HD), BF16),
        V((NC, NB, WR, 3 * HD), BF16),
        V((2, NB, BR, C), BF16),
        V((NB, 2, BR, C), BF16),
        V((NB * 2 * BR, C), F32),
        V((G, 2, 2, NB, C), BF16),
        V((G, 2, 2, NB, C), BF16),
        V((G, 8, C), F32),
        V((NB, 8, C), F32),
        V((NZ, NC, T, C), BF16),
        V((NC, T, C), F32),
        V((T, C), BF16),
        V((T, C), BF16),
        V((T, C), BF16),
        V((T, C), BF16),
        V((C, 2 * HD), BF16),
        V((HD, C), F32),
    ]
    dma = pltpu.SemaphoreType.DMA
    buffers.append(dma((8,)))
    buffers += [dma] * (2 * 16)
    buffers += [dma, dma((NZ,)), dma, dma]
    return buffers


def finish(npt_ref, pg_ref, wag_ref, small_ref, npt_o, pg_o, wg_o, bg_o, cg_o, og_o):
    N = npt_o.shape[1]
    npt_o[...] = npt_ref[...].reshape(2, N, C)
    pg_o[...] = pg_ref[...].reshape(2, N, C)
    scale = 1.0 / N
    width = HD // wag_ref.shape[0]
    cores = [wag_ref[i].astype(F32).reshape(C, 3 * HD) * scale for i in range(2)]
    pairs = [[v[:, i * HD : (i + 1) * HD] for v in cores] for i in range(2)]
    swapped = [[pltpu.roll(v, width, 1) for v in pair] for pair in pairs]
    first = lax.broadcasted_iota(jnp.int32, (C, HD), 1) < width
    wg_o[:, 0:HD] = jnp.where(first, pairs[0][0], pairs[0][1])
    wg_o[:, HD : 2 * HD] = jnp.where(first, pairs[1][0], swapped[1][1])
    wg_o[:, 2 * HD : 3 * HD] = jnp.where(first, swapped[1][0], pairs[1][1])
    wg_o[:, 3 * HD :] = jnp.where(first, swapped[0][0], swapped[0][1])
    og_o[...] = jnp.concatenate([v[0:width, 2 * HD :] for v in cores], axis=0)
    bg_o[...] = small_ref[0:H, :]
    cg_o[...] = small_ref[H : H + 1, 0:H]


def body(
    grid, pair, token_mask, chain_ids, proj_weight, bias_weight, chain_weight, out_weight, cotangent
):
    N = pair.shape[1]
    NY, NX, NZ, NC = grid
    vmem = pl.BlockSpec(memory_space=pltpu.VMEM)
    hbm = pl.BlockSpec(memory_space=pl.ANY)
    results = pl.pallas_call(
        functools.partial(kernel, grid, N),
        out_shape=(
            pltpu.VMEM((2 * N, C), F32),
            pltpu.VMEM((2 * N, C), BF16),
            pltpu.VMEM((NC, NX * NY, 128 // (NX * NY), 3 * HD), BF16),
            pltpu.VMEM((8, C), F32),
        ),
        in_specs=[hbm] * 8,
        out_specs=(vmem,) * 4,
        scratch_shapes=scratch(grid, N),
        compiler_params=pltpu.CompilerParams(collective_id=0, has_side_effects=True),
    )(
        chain_weight.reshape(1, H),
        pair,
        token_mask.reshape(1, N),
        chain_ids.reshape(1, N),
        proj_weight,
        jnp.transpose(bias_weight),
        out_weight,
        cotangent,
    )
    npt, pair_grad, weight_grad, bias_grad, chain_grad, out_grad = pl.pallas_call(
        finish,
        out_shape=(
            jax.ShapeDtypeStruct((2, N, C), F32),
            jax.ShapeDtypeStruct((2, N, C), BF16),
            jax.ShapeDtypeStruct((C, 4 * HD), F32),
            jax.ShapeDtypeStruct((H, C), F32),
            jax.ShapeDtypeStruct((1, H), F32),
            jax.ShapeDtypeStruct((HD, C), F32),
        ),
        in_specs=[vmem] * 4,
        out_specs=(vmem,) * 6,
    )(*[pltpu.with_memory_space_constraint(r, pltpu.VMEM) for r in results])
    return (
        npt,
        pair_grad,
        weight_grad,
        jnp.transpose(bias_grad),
        chain_grad.reshape(H),
        out_grad,
    )


def solution(mesh, grid=GRID):
    return jax.shard_map(
        functools.partial(body, grid),
        mesh=mesh,
        in_specs=(
            P(("dp", "dap"), None, None),
            P("dp"),
            P("dp"),
            P(),
            P(),
            P(),
            P(),
            P(("dp", "dap"), None, None),
        ),
        out_specs=(
            P(("dp", "dap"), None, None),
            P(("dp", "dap"), None, None),
            P("dp", None),
            P("dp", None),
            P("dp"),
            P("dp", None),
        ),
        check_vma=False,
    )
```

```python
import functools

import jax
import jax.numpy as jnp
from jax import lax
from jax.experimental import pallas as pl
from jax.experimental.pallas import tpu as pltpu
from jax.sharding import PartitionSpec as P

H = 4
DH = 32
HD = 128
C = 128
GRID = (4, 4, 4, 2)
EPSILON = 1e-05

F32 = jnp.float32
BF16 = jnp.bfloat16
NN = (((1,), (0,)), ((), ()))
NT = (((1,), (1,)), ((), ()))
TN = (((0,), (0,)), ((), ()))


def dot(a, b, dims=NN):
    return lax.dot_general(a, b, dims, preferred_element_type=F32)


def kernel(
    grid,
    tokens,
    cw_hbm,
    pair_hbm,
    mask_hbm,
    chain_hbm,
    w_hbm,
    bw_hbm,
    ow_hbm,
    cot_hbm,
    npt_o,
    pg_o,
    wag_o,
    small_o,
    cw_ref,
    pair_ref,
    mask_ref,
    chain_ref,
    w_ref,
    bw_ref,
    ow_ref,
    cot_ref,
    std_ref,
    inv_ref,
    q_ref,
    k_ref,
    v_ref,
    da_ref,
    qt_ref,
    dat_ref,
    gate_ref,
    dgate_ref,
    att_ref,
    dq_ref,
    dkv_ref,
    same_ref,
    dbias_ref,
    dproj_ref,
    s0_ref,
    dp_ref,
    slot_ref,
    bias_ref,
    sa_ref,
    ra_ref,
    sz_ref,
    rz_ref,
    wsa_ref,
    wra_ref,
    wrz_ref,
    wag_ref,
    us_ref,
    ub_ref,
    ux_ref,
    uz_ref,
    ur_ref,
    t0_ref,
    t1_ref,
    rows_ref,
    u32_ref,
    u16_ref,
    up_ref,
    d16_ref,
    dn_ref,
    wc_ref,
    nt_ref,
    ct_ref,
    in_s,
    slot_s,
    slot_r,
    ag_s,
    ag_r,
    rsa_s,
    rsa_r,
    rsz_s,
    rsz_r,
    wa_s,
    wa_r,
    wz_s,
    wz_r,
    wga_s,
    wga_r,
    wgc_s,
    wgc_r,
    ua_s,
    ua_r,
    uz_s,
    uz_r,
    t0_s,
    t0_r,
    t1_s,
    t1_r,
    pn_s,
    pn_r,
    pc_s,
    pc_r,
    up_s,
    up_r,
    dn_s,
    dn_r,
    nz_s,
    nz_r,
    nc_s,
    nc_r,
):
    NY, NX, NZ, NC = grid
    G = NZ * NC
    NB = NX * NY
    BR = 2 * G
    N = tokens
    T = 2 * N
    HC = H // NC

    idx = lax.axis_index("dap")
    zc = lax.rem(idx, G)
    c = lax.rem(idx, NC)
    z = lax.div(zc, NC)
    yx = lax.div(idx, G)
    x = lax.rem(yx, NX)
    y = lax.div(yx, NX)
    partner = idx + 1 - 2 * c
    near = HC * c
    HW = HC * DH

    def zc_peer(g):
        return idx + g - zc

    def yx_peer(b):
        return idx + (b - yx) * G

    def z_peer(zz):
        return idx + (zz - z) * NC

    def others(me, n):
        return [lax.rem(me + d, n) for d in range(1, n)]

    steps = [(i, j) for i in range(NY) for j in range(NX) if i or j]
    steps.sort(key=lambda s: -min(s[0], NY - s[0]) - min(s[1], NX - s[1]))
    plane = [lax.rem(y + i, NY) * NX + lax.rem(x + j, NX) for i, j in steps]
    reach = list(range(1, G))
    reach.sort(key=lambda d: -min(d // NC, NZ - d // NC))
    column = [lax.rem(zc - c + d - d % NC, G) + lax.rem(c + d, NC) for d in reach]

    def copy(src, dst, ssem, rsem, dev):
        return pltpu.make_async_remote_copy(
            src_ref=src,
            dst_ref=dst,
            send_sem=ssem,
            recv_sem=rsem,
            device_id={"dap": dev},
            device_id_type=pl.DeviceIdType.MESH,
        )

    drains = []

    def send(src, dst, ssem, rsem, dev):
        copy(src, dst, ssem, rsem, dev).start()

    def arrived(ref, sem):
        copy(ref, ref, sem, sem, partner).wait_recv()

    def later(ref, sem):
        drains.append(copy(ref, ref, sem, sem, partner))

    barrier = pltpu.get_barrier_semaphore()
    peers = [zc_peer(g) for g in column] + [yx_peer(b) for b in plane]
    for p in peers:
        pl.semaphore_signal(
            barrier, inc=1, device_id={"dap": p}, device_id_type=pl.DeviceIdType.MESH
        )

    loads = []
    for number, (src, dst) in enumerate(
        (
            (pair_hbm, pair_ref),
            (bw_hbm, bw_ref),
            (w_hbm, w_ref),
            (cot_hbm, cot_ref.at[c]),
            (ow_hbm, ow_ref),
            (chain_hbm, chain_ref),
            (mask_hbm, mask_ref),
            (cw_hbm, cw_ref),
        )
    ):
        d = pltpu.make_async_copy(src, dst, in_s.at[number])
        d.start()
        loads.append(d)
    loads[0].wait()

    values = pair_ref[...].reshape(T, C).astype(F32)
    centered = values - jnp.mean(values, axis=-1, keepdims=True)
    inverse = lax.rsqrt(jnp.mean(centered * centered, axis=-1, keepdims=True) + EPSILON)
    standard = centered * inverse
    std_ref[...] = standard
    inv_ref[...] = jnp.broadcast_to(inverse, (T, C))
    normed = standard.astype(BF16)
    rows_ref[z, c] = normed
    loads[1].wait()
    bwt = jnp.concatenate([bw_ref[...].astype(F32), jnp.zeros((8 - H, C), F32)], axis=0)
    bwt = bwt.astype(BF16)
    local_bias = dot(bwt, normed, NT)
    slot_ref[zc] = jnp.concatenate(
        [local_bias[0:H, 0:N], local_bias[0:H, N:T]], axis=0
    ).astype(BF16)

    pl.semaphore_wait(barrier, len(peers))
    for g in column:
        send(slot_ref.at[zc], slot_ref.at[zc], slot_s, slot_r, zc_peer(g))
    later(slot_ref.at[pl.ds(0, G - 1)], slot_s)
    part = rows_ref.at[z, c]
    send(part, part, pn_s, pn_r, partner)
    later(part, pn_s)
    for d in loads[2:]:
        d.wait()
    send(cot_ref.at[c], cot_ref.at[c], pc_s, pc_r, partner)
    later(cot_ref.at[c], pc_s)

    scaling = DH ** (-0.5)

    def project(core):
        projected = dot(rows_ref[z, core], w_ref[...])
        q32 = projected[:, 0:HD] * scaling
        q_ref[core] = q32.astype(BF16)
        k_ref[core] = projected[:, HD : 2 * HD].astype(BF16)
        v_ref[core] = projected[:, 2 * HD : 3 * HD].astype(BF16)
        gating = jax.nn.sigmoid(projected[:, 3 * HD :])
        gate_ref[core] = gating
        d_gated = dot(cot_ref[core].reshape(T, C), ow_ref[...], NT)
        da32 = d_gated * gating
        dgate_ref[core] = da32 * (1.0 - gating)
        da_ref[core] = da32.astype(BF16)
        for r in range(2):
            rows = slice(r * N, (r + 1) * N)
            qt_ref[core, r] = jnp.transpose(q32[rows]).astype(BF16)
            dat_ref[core, r] = jnp.transpose(da32[rows]).astype(BF16)

    project(c)
    arrived(rows_ref.at[z, 1 - c], pn_r)
    arrived(cot_ref.at[1 - c], pc_r)
    project(1 - c)
    for core in range(NC):
        rows = slice(core * T, (core + 1) * T)
        nt_ref[:, rows] = jnp.transpose(rows_ref[z, core].astype(F32)).astype(BF16)
        grads = cot_ref[core].reshape(T, C).astype(F32)
        ct_ref[:, rows] = jnp.transpose(grads).astype(BF16)

    part = rows_ref.at[z, c]
    round_z = [lax.rem(z + d, NZ) for d in ((2, 1, 3) if NZ == 4 else range(1, NZ))]
    for number, zz in enumerate(round_z):
        send(part, part, nz_s, nz_r.at[number], z_peer(zz))
    later(rows_ref.at[pl.ds(0, NZ - 1), c], nz_s)

    def row_slot(zz):
        part = rows_ref.at[zz, c]
        send(part, part, nc_s, nc_r, partner)

    chain = chain_ref[...].astype(F32)
    chain_cols = jnp.transpose(jnp.broadcast_to(chain, (HD, N)))
    chain_cols = jnp.concatenate([chain_cols] * (-(-N // HD)), axis=1)[:, 0:N]
    same_ref[...] = (chain_cols == jnp.broadcast_to(chain, (N, N))).astype(F32)
    masked = (mask_ref[...].astype(F32) - 1.0) * 1000000000.0
    head_of = lax.broadcasted_iota(jnp.int32, (N, HD), 1) // DH
    none = jnp.zeros((N, HD), BF16)

    @pl.loop(0, HC)
    def _(t):
        h = near + t
        own = head_of == h
        lane = lax.broadcasted_iota(jnp.int32, (1, H), 1) == h
        weight = jnp.sum(jnp.where(lane, cw_ref[...], 0.0), axis=1, keepdims=True)
        extra = weight * same_ref[...] + masked
        for core in range(NC):
            for r in range(2):
                rows = slice(r * N, (r + 1) * N)
                query = jnp.where(own, q_ref[core, rows, :], none)
                s0_ref[t, core, r] = dot(query, k_ref[core, rows, :], NT) + extra
                grad = jnp.where(own, da_ref[core, rows, :], none)
                dp_ref[t, core, r] = dot(grad, v_ref[core, rows, :], NT)

    arrived(slot_ref.at[pl.ds(0, G - 1)], slot_r)
    gathered = slot_ref[...].reshape(G * 2 * H, N)
    for t in range(HC):
        at = lax.broadcasted_iota(jnp.int32, (BR, G * 2 * H), 0) * H + (near + t)
        pick = (at == lax.broadcasted_iota(jnp.int32, (BR, G * 2 * H), 1)).astype(BF16)
        bias_ref[t, yx] = dot(pick, gathered).astype(BF16)

    for t in range(HC):
        part = bias_ref.at[t, yx]
        for b in plane:
            send(part, part, ag_s, ag_r.at[t], yx_peer(b))
    later(bias_ref.at[:, pl.ds(0, NB - 1)], ag_s)

    att_ref[...] = jnp.zeros((NC, 2, N, HD), F32)
    dq_ref[...] = jnp.zeros((NC, 2, N, HD), F32)

    @pl.loop(0, HC)
    def _(t):
        arrived(bias_ref.at[t, pl.ds(0, NB - 1)], ag_r.at[t])
        h = near + t
        own = head_of == h
        bias = bias_ref[t].reshape(N, N).astype(F32)
        head_rows = pl.ds(pl.multiple_of(h * DH, DH), DH)
        key_rows = pl.ds(pl.multiple_of(t * DH, DH), DH)
        value_rows = pl.ds(pl.multiple_of(HW + t * DH, DH), DH)
        for core in range(NC):
            for r in range(2):
                rows = slice(r * N, (r + 1) * N)
                scores = s0_ref[t, core, r] + bias
                expo = jnp.exp(scores - jnp.max(scores, axis=1, keepdims=True))
                probs = expo * (1.0 / jnp.sum(expo, axis=1, keepdims=True))
                probs_low = probs.astype(BF16)
                values = jnp.where(own, v_ref[core, rows, :], none)
                att_ref[core, r] += dot(probs_low, values)
                d_probs = dp_ref[t, core, r]
                inner = jnp.sum(probs * d_probs, axis=1, keepdims=True)
                d_scores = probs * (d_probs - inner)
                low = d_scores.astype(BF16)
                dq_ref[core, r] += dot(low, jnp.where(own, k_ref[core, rows, :], none))
                dkv_ref[core, r, key_rows, :] = dot(qt_ref[core, r, head_rows, :], low)
                dkv_ref[core, r, value_rows, :] = dot(
                    dat_ref[core, r, head_rows, :], probs_low
                )
                if core == 0 and r == 0:
                    dbias_ref[t] = d_scores
                else:
                    dbias_ref[t] += d_scores
        sa_ref[t] = dbias_ref[t].reshape(NB, BR, N).astype(BF16)
        for b in plane:
            send(sa_ref.at[t, b], ra_ref.at[yx, t], rsa_s, rsa_r, yx_peer(b))

    later(ra_ref.at[pl.ds(0, NB - 1)], rsa_s)

    rows_all = NC * T
    attended = att_ref[...].reshape(rows_all, HD)
    gating = gate_ref[...].reshape(rows_all, HD)
    gated = (gating * attended).astype(BF16)
    d_gate = dgate_ref[...].reshape(rows_all, HD) * attended
    d_query = dq_ref[...].reshape(rows_all, HD) * scaling
    mine = lax.broadcasted_iota(jnp.int32, (rows_all, HD), 1) // HW == c
    both = jnp.where(mine, d_query, pltpu.roll(d_gate, HW, 1))
    dproj_ref[:, 0:HD] = both.astype(BF16)
    for core in range(NC):
        for r in range(2):
            rows = slice((core * 2 + r) * N, (core * 2 + r + 1) * N)
            dproj_ref[rows, HD:] = jnp.transpose(dkv_ref[core, r]).astype(BF16)
    proj_part = dot(nt_ref[...], dproj_ref[...])
    out_part = dot(ct_ref[...], gated)
    wsa_ref[:, :, 0 : 2 * HD] = proj_part.reshape(NB, C // NB, 2 * HD).astype(BF16)
    wsa_ref[:, :, 2 * HD :] = out_part.reshape(NB, C // NB, HD).astype(BF16)
    for b in plane:
        send(wsa_ref.at[b], wra_ref.at[yx], wa_s, wa_r, yx_peer(b))
    later(wra_ref.at[pl.ds(0, NB - 1)], wa_s)
    wra_ref[yx] = wsa_ref[yx]

    update = dot(gated, ow_ref[...])
    u32_ref[...] = update.reshape(NC, T, C)
    u16_ref[...] = u32_ref[1 - c].astype(BF16)
    send(u16_ref, up_ref, up_s, up_r, partner)
    later(u16_ref, up_s)

    chain_sums = jnp.zeros((8, C), F32)
    lane = lax.broadcasted_iota(jnp.int32, (8, C), 1)
    row = lax.broadcasted_iota(jnp.int32, (8, C), 0)
    for t in range(HC):
        value = jnp.sum(dbias_ref[t] * same_ref[...], axis=0, keepdims=True)
        value = jnp.sum(value, axis=1, keepdims=True)
        chain_sums = jnp.where((row == H) & (lane == near + t), value, chain_sums)

    arrived(up_ref, up_r)
    update = u32_ref[c] + up_ref[...].astype(F32)
    next_pair = pair_ref[...].reshape(T, C).astype(F32) + update
    us_ref[...] = next_pair.astype(BF16).reshape(2, NB, BR, C)
    for b in plane:
        send(us_ref.at[:, b], ub_ref.at[yx], ua_s, ua_r, yx_peer(b))
    later(ub_ref.at[pl.ds(0, NB - 1)], ua_s)
    ub_ref[yx] = us_ref[:, yx]

    for number, d in enumerate((2, 3, 1) if NZ == 4 else range(NZ - 1, 0, -1)):
        zz = lax.rem(z + d, NZ)
        arrived(rows_ref.at[zz, c], nz_r.at[number])
        row_slot(zz)
    later(rows_ref.at[pl.ds(0, NZ - 1), c], nc_s)

    total = sa_ref[:, yx].astype(F32)
    arrived(ra_ref.at[pl.ds(0, NB - 1)], rsa_r)
    for b in plane:
        total = total + ra_ref[b].astype(F32)
    for g in range(G):
        for jl in range(2):
            sz_ref[g, jl * HC : (jl + 1) * HC, :] = total[:, 2 * g + jl, :]

    arrived(wra_ref.at[pl.ds(0, NB - 1)], wa_r)
    wsum = wra_ref[0].astype(F32)
    for b in range(1, NB):
        wsum = wsum + wra_ref[b].astype(F32)
    wrz_ref[z] = wsum.astype(BF16)
    for zz in others(z, NZ):
        send(wrz_ref.at[z], wrz_ref.at[z], wz_s, wz_r, z_peer(zz))
    later(wrz_ref.at[pl.ds(0, NZ - 1)], wz_s)

    wide = jnp.concatenate([total[:, i, :] for i in range(BR)], axis=1)
    row = lax.broadcasted_iota(jnp.int32, (8, BR * N), 0)
    parts = jnp.zeros((8, BR * N), F32)
    for t in range(HC):
        parts = jnp.where(row == near + t, wide[t : t + 1], parts)
    arrived(rows_ref.at[pl.ds(0, NZ - 1), 1 - c], nc_r)
    small = dot(parts.astype(BF16), rows_ref[...].reshape(BR * N, C))
    t0_ref[zc] = small + chain_sums
    for g in column:
        send(t0_ref.at[zc], t0_ref.at[zc], t0_s, t0_r, zc_peer(g))
    later(t0_ref.at[pl.ds(0, G - 1)], t0_s)

    for g in column:
        send(sz_ref.at[g], rz_ref.at[zc], rsz_s, rsz_r, zc_peer(g))
    later(rz_ref.at[pl.ds(0, G - 1)], rsz_s)
    rz_ref[zc] = sz_ref[zc]

    arrived(ub_ref.at[pl.ds(0, NB - 1)], ua_r)
    ux_ref[...] = ub_ref[...].reshape(NB * 2 * BR, C).astype(F32)
    for g in range(G):
        for jl in range(2):
            for r in range(2):
                start = r * BR + 2 * g + jl
                uz_ref[g, jl, r] = ux_ref[pl.ds(start, NB, stride=2 * BR), :].astype(BF16)
    for g in column:
        send(uz_ref.at[g], ur_ref.at[zc], uz_s, uz_r, zc_peer(g))
    later(ur_ref.at[pl.ds(0, G - 1)], uz_s)
    ur_ref[zc] = uz_ref[zc]

    first = lax.broadcasted_iota(jnp.int32, (C, HD), 1) < HW
    own_lanes = lax.broadcasted_iota(jnp.int32, (C, HD), 1) // HW == c
    weights = [w_ref[:, i * HD : (i + 1) * HD].astype(F32) for i in range(4)]
    swapped = [pltpu.roll(v, HW, 1) for v in weights]
    pick_k = jnp.where(c == 0, weights[1], swapped[1])
    pick_v = jnp.where(c == 0, swapped[2], weights[2])
    wc_ref[:, 0:HD] = jnp.where(own_lanes, weights[0], swapped[3]).astype(BF16)
    wc_ref[:, HD:] = jnp.where(first, pick_k, pick_v).astype(BF16)
    u32_ref[...] = dot(dproj_ref[...], wc_ref[...], NT).reshape(NC, T, C)
    d16_ref[...] = u32_ref[1 - c].astype(BF16)
    send(d16_ref, dn_ref, dn_s, dn_r, partner)
    later(d16_ref, dn_s)

    arrived(wrz_ref.at[pl.ds(0, NZ - 1)], wz_r)
    wsum = wrz_ref[0].astype(F32)
    for zz in range(1, NZ):
        wsum = wsum + wrz_ref[zz].astype(F32)
    wag_ref[c, yx] = wsum.astype(BF16)

    part = wag_ref.at[c, yx]
    half = NB // 2
    for number, b in enumerate(plane):
        send(part, part, wga_s, wga_r.at[number // half], yx_peer(b))
    later(wag_ref.at[c, pl.ds(0, NB - 1)], wga_s)

    def pass_on(b):
        part = wag_ref.at[c, b]
        send(part, part, wgc_s, wgc_r, partner)

    pass_on(yx)

    arrived(t0_ref.at[pl.ds(0, G - 1)], t0_r)
    small = t0_ref[0]
    for g in range(1, G):
        small = small + t0_ref[g]
    t1_ref[yx] = small
    for b in plane:
        send(t1_ref.at[yx], t1_ref.at[yx], t1_s, t1_r, yx_peer(b))
    later(t1_ref.at[pl.ds(0, NB - 1)], t1_s)

    arrived(rz_ref.at[pl.ds(0, G - 1)], rsz_r)
    sums = []
    for core in range(NC):
        part = rz_ref[core]
        for zz in range(1, NZ):
            part = part + rz_ref[zz * NC + core]
        sums.append(part)
    d_bias = []
    for jl in range(2):
        d_bias.append(
            jnp.concatenate([s[jl * HC : (jl + 1) * HC] for s in sums], axis=0)
        )
    d_bias = jnp.concatenate(d_bias, axis=1)
    d_bias = jnp.concatenate([d_bias, jnp.zeros((8 - H, T), F32)], axis=0).astype(BF16)

    arrived(dn_ref, dn_r)
    d_normed = u32_ref[c] + dn_ref[...].astype(F32) + dot(d_bias, bwt, TN)
    standard = std_ref[...]
    mean_grad = jnp.mean(d_normed, axis=-1, keepdims=True)
    mean_cross = jnp.mean(d_normed * standard, axis=-1, keepdims=True)
    pair_grad = (d_normed - mean_grad - standard * mean_cross) * inv_ref[...]
    pg_o[...] = pair_grad.astype(BF16).reshape(2, N, C)

    back = [lax.rem(y - i + NY, NY) * NX + lax.rem(x - j + NX, NX) for i, j in steps]
    for group in (1, 0):
        blocks = back[group * half : (group + 1) * half]
        arrived(wag_ref.at[c, pl.ds(0, len(blocks))], wga_r.at[group])
        for b in blocks:
            pass_on(b)
    later(wag_ref.at[c], wgc_s)

    arrived(ur_ref.at[pl.ds(0, G - 1)], uz_r)
    for g in range(G):
        for jl in range(2):
            for r in range(2):
                start = 2 * g + r
                npt_o[jl, pl.ds(start, NB, stride=BR), :] = ur_ref[g, jl, r].astype(F32)

    arrived(t1_ref.at[pl.ds(0, NB - 1)], t1_r)
    small = t1_ref[0]
    for b in range(1, NB):
        small = small + t1_ref[b]
    small_o[...] = small * (1.0 / N)
    arrived(wag_ref.at[1 - c], wgc_r)
    wag_o[...] = wag_ref[...]

    for d in drains:
        d.wait_send()


def scratch(grid, N):
    NY, NX, NZ, NC = grid
    G, NB, HC = NZ * NC, NX * NY, H // NC
    BR, T, WR = 2 * G, 2 * N, 128 // NB
    V = pltpu.VMEM
    buffers = [
        V((1, H), F32),
        V((2, N, C), BF16),
        V((1, N), jnp.int32),
        V((1, N), jnp.int32),
        V((C, 4 * HD), BF16),
        V((H, C), BF16),
        V((HD, C), BF16),
        V((NC, 2, N, C), BF16),
        V((T, C), F32),
        V((T, C), F32),
        V((NC, T, HD), BF16),
        V((NC, T, HD), BF16),
        V((NC, T, HD), BF16),
        V((NC, T, HD), BF16),
        V((NC, 2, HD, N), BF16),
        V((NC, 2, HD, N), BF16),
        V((NC, T, HD), F32),
        V((NC, T, HD), F32),
        V((NC, 2, N, HD), F32),
        V((NC, 2, N, HD), F32),
        V((NC, 2, HD, N), F32),
        V((N, N), F32),
        V((HC, N, N), F32),
        V((NC * T, 2 * HD), BF16),
        V((HC, NC, 2, N, N), F32),
        V((HC, NC, 2, N, N), F32),
        V((G, 2 * H, N), BF16),
        V((HC, NB, BR, N), BF16),
        V((HC, NB, BR, N), BF16),
        V((NB, HC, BR, N), BF16),
        V((G, 2 * HC, N), F32),
        V((G, 2 * HC, N), F32),
        V((NB, WR, 3 * HD), BF16),
        V((NB, WR, 3 * HD), BF16),
        V((NZ, WR, 3 * HD), BF16),
        V((NC, NB, WR, 3 * HD), BF16),
        V((2, NB, BR, C), BF16),
        V((NB, 2, BR, C), BF16),
        V((NB * 2 * BR, C), F32),
        V((G, 2, 2, NB, C), BF16),
        V((G, 2, 2, NB, C), BF16),
        V((G, 8, C), F32),
        V((NB, 8, C), F32),
        V((NZ, NC, T, C), BF16),
        V((NC, T, C), F32),
        V((T, C), BF16),
        V((T, C), BF16),
        V((T, C), BF16),
        V((T, C), BF16),
        V((C, 2 * HD), BF16),
        V((C, NC * T), BF16),
        V((C, NC * T), BF16),
    ]
    dma = pltpu.SemaphoreType.DMA
    buffers.append(dma((8,)))
    singles = [dma] * (2 * 16)
    singles[3] = dma((HC,))
    singles[13] = dma((2,))
    buffers += singles
    buffers += [dma, dma((NZ,)), dma, dma]
    return buffers


def finish(npt_ref, pg_ref, wag_ref, small_ref, npt_o, pg_o, wg_o, bg_o, cg_o, og_o):
    N = npt_o.shape[1]
    npt_o[...] = npt_ref[...]
    pg_o[...] = pg_ref[...]
    scale = 1.0 / N
    width = HD // wag_ref.shape[0]
    cores = [wag_ref[i].astype(F32).reshape(C, 3 * HD) * scale for i in range(2)]
    pairs = [[v[:, i * HD : (i + 1) * HD] for v in cores] for i in range(2)]
    swapped = [[pltpu.roll(v, width, 1) for v in pair] for pair in pairs]
    first = lax.broadcasted_iota(jnp.int32, (C, HD), 1) < width
    wg_o[:, 0:HD] = jnp.where(first, pairs[0][0], pairs[0][1])
    wg_o[:, HD : 2 * HD] = jnp.where(first, pairs[1][0], swapped[1][1])
    wg_o[:, 2 * HD : 3 * HD] = jnp.where(first, swapped[1][0], pairs[1][1])
    wg_o[:, 3 * HD :] = jnp.where(first, swapped[0][0], swapped[0][1])
    out_t = jnp.where(first, cores[0][:, 2 * HD :], cores[1][:, 2 * HD :])
    og_o[...] = jnp.transpose(out_t)
    bg_o[...] = small_ref[0:H, :]
    cg_o[...] = small_ref[H : H + 1, 0:H]


def body(
    grid, pair, token_mask, chain_ids, proj_weight, bias_weight, chain_weight, out_weight, cotangent
):
    N = pair.shape[1]
    NY, NX, NZ, NC = grid
    vmem = pl.BlockSpec(memory_space=pltpu.VMEM)
    hbm = pl.BlockSpec(memory_space=pl.ANY)
    results = pl.pallas_call(
        functools.partial(kernel, grid, N),
        out_shape=(
            pltpu.VMEM((2, N, C), F32),
            pltpu.VMEM((2, N, C), BF16),
            pltpu.VMEM((NC, NX * NY, 128 // (NX * NY), 3 * HD), BF16),
            pltpu.VMEM((8, C), F32),
        ),
        in_specs=[hbm] * 8,
        out_specs=(vmem,) * 4,
        scratch_shapes=scratch(grid, N),
        compiler_params=pltpu.CompilerParams(collective_id=0, has_side_effects=True),
    )(
        chain_weight.reshape(1, H),
        pair,
        token_mask.reshape(1, N),
        chain_ids.reshape(1, N),
        proj_weight,
        jnp.transpose(bias_weight),
        out_weight,
        cotangent,
    )
    npt, pair_grad, weight_grad, bias_grad, chain_grad, out_grad = pl.pallas_call(
        finish,
        out_shape=(
            jax.ShapeDtypeStruct((2, N, C), F32),
            jax.ShapeDtypeStruct((2, N, C), BF16),
            jax.ShapeDtypeStruct((C, 4 * HD), F32),
            jax.ShapeDtypeStruct((H, C), F32),
            jax.ShapeDtypeStruct((1, H), F32),
            jax.ShapeDtypeStruct((HD, C), F32),
        ),
        in_specs=[vmem] * 4,
        out_specs=(vmem,) * 6,
    )(*[pltpu.with_memory_space_constraint(r, pltpu.VMEM) for r in results])
    return (
        npt,
        pair_grad,
        weight_grad,
        jnp.transpose(bias_grad),
        chain_grad.reshape(H),
        out_grad,
    )


def solution(mesh, grid=GRID):
    return jax.shard_map(
        functools.partial(body, grid),
        mesh=mesh,
        in_specs=(
            P(("dp", "dap"), None, None),
            P("dp"),
            P("dp"),
            P(),
            P(),
            P(),
            P(),
            P(("dp", "dap"), None, None),
        ),
        out_specs=(
            P(("dp", "dap"), None, None),
            P(("dp", "dap"), None, None),
            P("dp", None),
            P("dp", None),
            P("dp"),
            P("dp", None),
        ),
        check_vma=False,
    )
```
